32 devices in a mesh: dp: 8 (over y, x, core), mp: 4 (over z).
Axes of the slice: x: 2, y: 2, z: 4, core: 2. Of those that a mesh axis runs over, the one named last changes fastest.
Arguments:
- tokens: bfloat16 [2048, 8192], P('dp', 'mp'), may hold values from -8 to 8
- attn_gain: bfloat16 [8192], replicated, may hold values from 0.5 to 1.5
- w_query: bfloat16 [8192, 4096], P('dp', 'mp'), may hold values from -2 to 2
- key_projection_weight: bfloat16 [8192, 512], P('dp', 'mp'), may hold values from -2 to 2
- value_projection_weight: bfloat16 [8192, 512], P('dp', 'mp'), may hold values from -0.0625 to 0.0625
- w_out: bfloat16 [4096, 8192], P('mp', 'dp'), may hold values from -0.09375 to 0.09375
- final_gain: bfloat16 [8192], P('mp'), may hold values from 0.5 to 1.5
- unembed: bfloat16 [64128, 8192], P('dp', 'mp'), may hold values from -0.29882812 to 0.29882812
- clean_ids: int32 [8], replicated, may hold values from 0 to 64127, as said below
- corrupt_ids: int32 [8], replicated, may hold values from 0 to 64127
Outputs:
- head_out: bfloat16 [2048, 4096], P('dp', 'mp')
- scores: float32 [8, 32], P('dp', 'mp')
- metric: float32 [8], P('dp')
The draws below stay inside these ranges and needn't reach their ends.
Inputs may be any that keep to these rules, and one draw needn't show every extreme that they name: `clean_ids`: split the ids into 8 aligned blocks of equal size and number the groups of 1 sequence alike; the block of a clean answer, minus the number of its sequence's group, taken modulo the number of blocks, is drawn so that every such offset occurs for some sequence.
All inputs are finite; a program needn't handle non-finite values.
Results may differ from the reference program's by a relative error of at most 0.015.
Values may be sent and summed in bfloat16 or wider, within the bound.
A program may use at most 128 MiB of HBM per device.

```python
import math
import jax
import jax.numpy as jnp
from jax import lax

MODEL_WIDTH = 8192
QUERY_HEADS = 32
KEY_VALUE_HEADS = 4
HEAD_SIZE = 128
VOCAB = 64128
SEQUENCE_LENGTH = 256
SEQ_DEV = 1
SEQS = 8
TOKENS = 2048


def draw_tokens(key, part):
    key_common, key_jitter, key_shared = jax.random.split(jax.random.fold_in(key, 7), 3)
    common = jax.random.normal(key_common, (1, 1, MODEL_WIDTH), jnp.float32)
    ramp_up = jnp.arange(SEQS, dtype=jnp.float32) / max(SEQS - 1, 1)
    jitter = jax.random.uniform(key_jitter, (SEQS,), jnp.float32, 0.7, 1.3)
    perturbation_scale = 0.3 * 10.0 ** ramp_up * jitter
    random_perturbation = jax.random.normal(key_shared, (SEQS, SEQUENCE_LENGTH, MODEL_WIDTH), jnp.float32)
    drawn = random_perturbation + perturbation_scale[:, None, None] * common
    return jnp.clip(drawn, -8.0, 8.0).reshape(TOKENS, MODEL_WIDTH).astype(jnp.bfloat16)


def paired_weights(key):
    random_key_for_key = jax.random.fold_in(jax.random.fold_in(key, 23), 0)
    key_query = jax.random.fold_in(jax.random.fold_in(key, 23), 3)
    key_matrix = jax.random.normal(random_key_for_key, (MODEL_WIDTH, KEY_VALUE_HEADS * HEAD_SIZE), jnp.float32) / math.sqrt(MODEL_WIDTH)
    query_matrix = jax.random.normal(key_query, (MODEL_WIDTH, QUERY_HEADS * HEAD_SIZE), jnp.float32) / math.sqrt(MODEL_WIDTH)
    return (jnp.clip(query_matrix, -2.0, 2.0), jnp.clip(key_matrix, -2.0, 2.0))


def draw_w_query(key, part):
    return paired_weights(key)[0].astype(jnp.bfloat16)


def draw_key_projection_weight(key, part):
    return paired_weights(key)[1].astype(jnp.bfloat16)


def draw_clean_ids(key, part):
    key_order, key_inner = jax.random.split(jax.random.fold_in(key, 41), 2)
    group_count = SEQS // SEQ_DEV
    block_size = VOCAB // group_count
    shuffled = jax.random.permutation(key_order, group_count).astype(jnp.int32)
    offsets = (shuffled - shuffled[0] + group_count - 1) % group_count
    seq_index = jnp.arange(SEQS, dtype=jnp.int32)
    owner = seq_index // SEQ_DEV
    block = (owner + offsets[seq_index % group_count]) % group_count
    inner = jax.random.randint(key_inner, (SEQS,), 0, block_size, jnp.int32)
    inner = jnp.where(seq_index == 0, block_size - 1, inner)
    return (block * block_size + inner).astype(jnp.int32)


def set_ends(values, key, smallest, top_value):
    dims = values.shape
    spot = [jax.random.randint(jax.random.fold_in(key, axis), (), 0, dims[axis]) for axis in range(len(dims))]
    values = values.at[tuple(spot)].set(smallest)
    longest = dims.index(max(dims))
    spot[longest] = (spot[longest] + 1) % dims[longest]
    return values.at[tuple(spot)].set(top_value)


def level_of(rng, dims, shards, low, top_value):
    def one(axis_at, parts):
        heights = jax.random.uniform(jax.random.fold_in(jax.random.fold_in(rng, 6), axis_at), (parts,), jnp.float32, low / len(shards), top_value / len(shards))
        return jnp.repeat(jnp.exp(heights), dims[axis_at] // parts).reshape((-1,) + (1,) * (len(dims) - axis_at - 1))

    loudness = one(*shards[0])
    for cut in shards[1:]:
        loudness = loudness * one(*cut)
    return loudness


def normal_values(stream_key, extent, width, bound, pieces=(), kind=jnp.bfloat16):
    factor_of = level_of(stream_key, extent, pieces, -0.22, 0.18) if pieces else 1.0
    values = jax.random.normal(stream_key, extent, jnp.float32) * width * factor_of
    return jnp.minimum(jnp.maximum(values, -bound), bound).astype(kind)


def setup_inputs(seed: int = 0) -> dict:
    arg_keys = jax.random.split(jax.random.key(seed), 11)
    tokens = draw_tokens(jax.random.fold_in(arg_keys[10], 71), 0)
    attn_gain = jnp.clip(1.0 + 0.1 * jax.random.normal(arg_keys[1], (MODEL_WIDTH,), jnp.float32), 0.5, 1.5).astype(jnp.bfloat16)
    w_query = draw_w_query(jax.random.fold_in(arg_keys[10], 71), 0)
    key_projection_weight = draw_key_projection_weight(jax.random.fold_in(arg_keys[10], 71), 0)
    value_projection_weight = normal_values(arg_keys[4], (MODEL_WIDTH, KEY_VALUE_HEADS * HEAD_SIZE), MODEL_WIDTH ** -0.5, 0.0625, ((0, 8), (1, 4)))
    w_out = normal_values(arg_keys[5], (QUERY_HEADS * HEAD_SIZE, MODEL_WIDTH), (QUERY_HEADS * HEAD_SIZE) ** -0.5, 0.09375, ((0, 4), (1, 8)))
    final_gain = jnp.clip(1.0 + 0.1 * jax.random.normal(arg_keys[6], (MODEL_WIDTH,), jnp.float32), 0.5, 1.5).astype(jnp.bfloat16)
    unembed = normal_values(arg_keys[7], (VOCAB, MODEL_WIDTH), 0.05, 0.29882812, ((0, 8), (1, 4)))
    clean_ids = draw_clean_ids(jax.random.fold_in(arg_keys[10], 71), 0)
    corrupt_ids = set_ends(jax.random.randint(arg_keys[9], (SEQS,), 0, VOCAB), jax.random.fold_in(arg_keys[9], 1), 0, VOCAB - 1).astype(jnp.int32)
    return dict(tokens=tokens, attn_gain=attn_gain, w_query=w_query, key_projection_weight=key_projection_weight, value_projection_weight=value_projection_weight, w_out=w_out, final_gain=final_gain, unembed=unembed, clean_ids=clean_ids, corrupt_ids=corrupt_ids)


def apply_rotary(tensor, length):
    half_dim = tensor.shape[-1] // 2
    positions = jnp.arange(length, dtype=jnp.float32)
    inv_freq = jnp.exp(jnp.arange(half_dim, dtype=jnp.float32) * (-2.0 * math.log(500000.0) / tensor.shape[-1]))
    angles = positions[:, None] * inv_freq[None, :]
    cosine_table = jnp.cos(angles)[:, None, :]
    sine_table = jnp.sin(angles)[:, None, :]
    lower_half = tensor[..., :half_dim]
    upper_half = tensor[..., half_dim:]
    return jnp.concatenate([lower_half * cosine_table - upper_half * sine_table, upper_half * cosine_table + lower_half * sine_table], axis=-1)

def attend(queries, projected_key_rows, value_rows):
    length, q_heads, head_dim = queries.shape
    kv_heads = projected_key_rows.shape[1]
    grouped = queries.reshape(length, kv_heads, q_heads // kv_heads, head_dim)
    logits = jnp.einsum('tkgd,skd->kgts', grouped.astype(jnp.float32), projected_key_rows.astype(jnp.float32)) / math.sqrt(head_dim)
    causal = jnp.arange(length)[:, None] >= jnp.arange(length)[None, :]
    logits = jnp.where(causal, logits, -1e+30)
    row_top = lax.optimization_barrier(jnp.max(logits, axis=-1, keepdims=True))
    exponent = jnp.exp(logits - row_top)
    attn_probs = (exponent / lax.optimization_barrier(jnp.sum(exponent, axis=-1, keepdims=True))).astype(jnp.bfloat16)
    mixed_heads = jnp.einsum('kgts,skd->tkgd', attn_probs.astype(jnp.float32), value_rows.astype(jnp.float32))
    return mixed_heads.astype(jnp.bfloat16).reshape(length, q_heads * head_dim)

def reference(tokens, attn_gain, w_query, key_projection_weight, value_projection_weight, w_out, final_gain, unembed, clean_ids, corrupt_ids):

    def one_sequence(tokens_seq):
        wide = tokens_seq.astype(jnp.float32)
        normalized_rows = (wide * lax.rsqrt(lax.optimization_barrier(jnp.mean(wide * wide, axis=1, keepdims=True)) + 1e-05) * attn_gain.astype(jnp.float32)).astype(jnp.bfloat16)
        queries = apply_rotary(jnp.dot(normalized_rows, w_query, preferred_element_type=jnp.float32).reshape(SEQUENCE_LENGTH, QUERY_HEADS, HEAD_SIZE), SEQUENCE_LENGTH).astype(jnp.bfloat16)
        projected_key_rows = apply_rotary(jnp.dot(normalized_rows, key_projection_weight, preferred_element_type=jnp.float32).reshape(SEQUENCE_LENGTH, KEY_VALUE_HEADS, HEAD_SIZE), SEQUENCE_LENGTH).astype(jnp.bfloat16)
        value_rows = jnp.dot(normalized_rows, value_projection_weight, preferred_element_type=jnp.float32).astype(jnp.bfloat16).reshape(SEQUENCE_LENGTH, KEY_VALUE_HEADS, HEAD_SIZE)
        return attend(queries, projected_key_rows, value_rows)
    per_seq = lax.map(one_sequence, tokens.reshape(SEQS, SEQUENCE_LENGTH, MODEL_WIDTH))
    head_out = per_seq.reshape(TOKENS, QUERY_HEADS * HEAD_SIZE)
    head_mean = lax.optimization_barrier(jnp.sum(head_out.astype(jnp.float32), axis=0)) / TOKENS
    last_out = per_seq[:, SEQUENCE_LENGTH - 1, :]
    attn_last = jnp.dot(last_out, w_out, preferred_element_type=jnp.float32).astype(jnp.bfloat16)
    residual = tokens.reshape(SEQS, SEQUENCE_LENGTH, MODEL_WIDTH)[:, SEQUENCE_LENGTH - 1, :].astype(jnp.float32) + attn_last.astype(jnp.float32)
    direction = unembed[clean_ids].astype(jnp.float32) - unembed[corrupt_ids].astype(jnp.float32)
    weighted = final_gain.astype(jnp.float32) * direction
    inverse = lax.rsqrt(lax.optimization_barrier(jnp.mean(residual * residual, axis=1)) + 1e-05)
    metric = inverse * lax.optimization_barrier(jnp.sum(residual * weighted, axis=1))
    grad_last = (weighted * inverse[:, None] - residual * (metric * inverse * inverse / MODEL_WIDTH)[:, None]).astype(jnp.bfloat16)
    head_grads = jnp.dot(grad_last, w_out.T, preferred_element_type=jnp.float32)
    mean_gap = head_mean[None, :] - last_out.astype(jnp.float32)
    scores = lax.optimization_barrier(jnp.sum((mean_gap * head_grads).reshape(SEQS, QUERY_HEADS, HEAD_SIZE), axis=2))
    return (head_out, scores, metric)
```

```python
import functools
import math

import jax
import jax.numpy as jnp
import numpy as np
from jax import lax
from jax.experimental import pallas as pl
from jax.experimental.pallas import tpu as pltpu
from jax.sharding import PartitionSpec as P

HEAD_SIZE = 128
SEQUENCE_LENGTH = 256
MESH = pl.DeviceIdType.MESH
F32 = jnp.float32
BF16 = jnp.bfloat16


def flip(index, mask):
    bit = 1
    out = index
    while bit <= mask:
        if mask & bit:
            out = out + bit - 2 * bit * ((index // bit) % 2)
        bit *= 2
    return out


def spread_plan(size):
    bits = []
    bit = 2
    while bit < size:
        bits.append(bit)
        bit *= 2
    parts = min(2, len(bits))
    plan = []
    for part in range(parts):
        order = bits[part:] + bits[:part]
        held = [0]
        arrivals = []
        for step, b in enumerate(order):
            fresh = [h ^ b for h in held]
            arrivals += [(f, step) for f in fresh]
            held = held + fresh
        plan.append((order, arrivals))
    return plan


def head_groups(heads, piece):
    if piece < 256 or heads < 4:
        return [heads]
    sizes = [2] * ((heads - 2) // 2)
    return sizes + [1] * (heads - sum(sizes))


def order_tasks(events, tasks):
    done = dict(events)
    left = dict(tasks)
    clock = 0.0
    out = []
    while left:
        ready = {
            name: max([0.0] + [done[dep] + lag for dep, lag in deps])
            for name, (deps, dur, rank, fn) in left.items()
            if all(dep in done for dep, lag in deps)
        }
        now = [name for name in ready if ready[name] <= clock]
        if not now:
            clock = min(ready.values())
            continue
        name = min(now, key=lambda n: (left[n][2], ready[n]))
        deps, dur, rank, fn = left.pop(name)
        out.append((clock, fn))
        clock += dur
        done[name] = clock
    return out


def whole_kernel(
    D, M, sizes, xchunks, token_count,
    tok_ref, gain_ref, wq_ref, wk_ref, wv_ref, cos_hbm, sin_hbm, wout_hbm, contrib_ref, fgain_ref,
    head_ref, scores_ref, metric_ref,
    *scratch,
):
    G_ = len(sizes) + 1
    w_bufs = scratch[:G_]
    (
        x_all, x_n, acc, gain_s, ss, cos_ref, sin_ref, wout_ref, tail_tok, q_s, k_s, v_s,
        dir_all, g_src, g_all, qp_src, qp_all, pre_w, pre_t, last_src, last_all, rows_a,
        out_src, out_all, hg_src, hg_all, tot_src, tot_all,
        loc_sem, one_sem, xs_sem, xr_sem, ps_sem, pr_sem, cs_sem, cr_sem,
        s1, r1, s2, r2, s3, r3, s4, r4, s6, r6, s7, r7, s8, r8,
    ) = scratch[G_:]
    d = lax.axis_index("dp")
    m = lax.axis_index("mp")
    plan = spread_plan(D)
    parts = len(plan)
    steps = len(plan[0][0])
    depth = wq_ref.shape[0]
    rows, width = tok_ref.shape
    qw, kw, vw = wq_ref.shape[1], wk_ref.shape[1], wv_ref.shape[1]
    piece = depth // parts
    xpiece = rows // xchunks
    L = SEQUENCE_LENGTH
    S = rows // L
    heads, kv_heads = qw // HEAD_SIZE, kw // HEAD_SIZE
    per_kv = heads // kv_heads
    cols = wout_ref.shape[1]
    R = D // M
    everyone = D * M
    me = d * M + m
    model_width = M * width
    home = d // R
    half = HEAD_SIZE // 2
    DS = D * S

    spans = [(qw, kw + vw)]
    head_span = [None]
    at = 0
    for n in sizes:
        spans.append((at * HEAD_SIZE, n * HEAD_SIZE))
        head_span.append((at, at + n))
        at += n
    ngroups = len(spans)

    def wref(owner, g, p):
        return w_bufs[g].at[owner // R, pl.ds((owner % R) * depth + p * piece, piece), :]

    own = {}
    for g in range(ngroups):
        for p in range(parts):
            rr = pl.ds(p * piece, piece)
            dst = wref(d, g, p)
            lo, n = spans[g]
            if g == 0:
                moves = [(wk_ref.at[rr, :], dst.at[:, pl.ds(0, kw)]),
                         (wv_ref.at[rr, :], dst.at[:, pl.ds(kw, vw)])]
            else:
                moves = [(wq_ref.at[rr, pl.ds(lo, n)], dst)]
            own[g, p] = [
                pltpu.make_async_copy(a, b, loc_sem.at[g, p, i]) for i, (a, b) in enumerate(moves)
            ]
            for cp in own[g, p]:
                cp.start()

    barrier = pltpu.get_barrier_semaphore()

    @pl.loop(1, everyone)
    def _(i):
        other = (me + i) % everyone
        pl.semaphore_signal(
            barrier, inc=1, device_id=(other // M, other % M), device_id_type=MESH
        )

    xown = pltpu.make_async_copy(tok_ref, x_all.at[m], one_sem.at[0])
    early = [
        pltpu.make_async_copy(cos_hbm, cos_ref, one_sem.at[1]),
        pltpu.make_async_copy(sin_hbm, sin_ref, one_sem.at[2]),
        pltpu.make_async_copy(wout_hbm, wout_ref, one_sem.at[3]),
    ]
    for b in range(S):
        early.append(pltpu.make_async_copy(
            tok_ref.at[pl.ds((b + 1) * L - 16, 16), :], tail_tok.at[b], one_sem.at[4 + b]
        ))
    xown.start()
    for cp in early:
        cp.start()
    for k in range(M):
        gain_s[k] = gain_ref[k * width:(k + 1) * width].astype(F32).reshape(1, width)
    ss[...] = jnp.zeros_like(ss)
    pl.semaphore_wait(barrier, everyone - 1)

    pending = []

    def remote(src, dst, send_sem, recv_sem, to, cond=None):
        cp = pltpu.make_async_remote_copy(
            src_ref=src, dst_ref=dst, send_sem=send_sem, recv_sem=recv_sem,
            device_id=to, device_id_type=MESH,
        )
        if cond is None:
            cp.start()
        else:
            pl.when(cond)(cp.start)
        pending.append((cp, cond))

    def local(src, dst, sem, cond=None):
        cp = pltpu.make_async_copy(src, dst, sem)
        if cond is None:
            cp.start()
        else:
            pl.when(cond)(cp.start)

    def arrive(buf, sem, n):
        for i in range(n):
            pltpu.make_async_copy(buf.at[i], buf.at[i], sem.at[i]).wait()

    def spread(src, dst, send_sem, recv_sem, same=False):
        for i in range(1, D):
            to = (d + i) % D
            remote(src if same else src.at[to], dst.at[d], send_sem.at[i], recv_sem.at[d], (to, m))
        local(src if same else src.at[d], dst.at[d], recv_sem.at[d])

    def xsend(hop, c, side):
        rr = pl.ds(c * xpiece, xpiece)
        owner = m - hop if side == 0 else m + hop
        to = m + 1 if side == 0 else m - 1
        return pltpu.make_async_remote_copy(
            src_ref=(tok_ref.at[rr, :] if hop == 0 else x_all.at[owner, rr, :]),
            dst_ref=x_all.at[owner, rr, :],
            send_sem=xs_sem.at[hop, c, side],
            recv_sem=xr_sem.at[hop, c, side],
            device_id=(d, to),
            device_id_type=MESH,
        )

    def xpred(hop, side):
        if side == 0:
            return (m < M - 1) & (m - hop >= 0)
        return (m > 0) & (m + hop < M)

    def xstart(hop, c):
        for side in range(2):
            @pl.when(xpred(hop, side))
            def _(side=side):
                xsend(hop, c, side).start()

    def xwait(hop, c):
        rr = pl.ds(c * xpiece, xpiece)
        for side in range(2):
            owner = m - hop - 1 if side == 0 else m + hop + 1
            ok = (m - hop - 1 >= 0) if side == 0 else (m + hop + 1 < M)

            @pl.when(ok)
            def _(side=side, owner=owner):
                pltpu.make_async_copy(
                    x_all.at[owner, rr, :], x_all.at[owner, rr, :], xr_sem.at[hop, c, side]
                ).wait()

    def wcopy(mask, g, p, bit, send_sem, recv_sem):
        ref = wref(flip(d, mask), g, p)
        remote(ref, ref, send_sem, recv_sem, (flip(d, bit), m))

    def wsend(mask, g, p, step):
        bit = plan[p][0][step]
        wcopy(mask, g, p, bit, ps_sem.at[p, mask // 2, g, step],
              pr_sem.at[p, (mask ^ bit) // 2, g])

    def csend(mask, g, p):
        wcopy(mask, g, p, 1, cs_sem.at[p, mask // 2, g], cr_sem.at[p, mask // 2, g])

    def wwait(mask, g, p, sem):
        ref = wref(flip(d, mask), g, p)
        pltpu.make_async_copy(ref, ref, sem).wait()

    def own_ready(g, p):
        for cp in own.pop((g, p), []):
            cp.wait()

    def own_sends(g):
        for p in range(parts):
            own_ready(g, p)
            wsend(0, g, p, 0)
        for step in range(1, steps):
            for p in range(parts):
                wsend(0, g, p, step)
        for p in range(parts):
            csend(0, g, p)

    pace = 46e3
    hops = len(plan[0][0])
    rounds = len(plan[0][1])
    shard_time = rows * width * 2 / pace
    group_time = [(D // 2 - 1) * depth * n * 2 / hops / pace for _, n in spans]
    share = hops / rounds
    own_at, rel_at = {}, {}
    clock = 0.0
    queue = [("own", 0)] + ([("own", 1)] if ngroups > 1 else [])
    for g in range(ngroups):
        queue.append(("rel", g))
        if g + 2 < ngroups:
            queue.append(("own", g + 2))
    for kind, g in queue:
        if kind == "own":
            own_at[g] = clock
            clock += group_time[g] * share
        else:
            clock += group_time[g] * (1 - share)
            rel_at[g] = clock

    timed = []
    events = {}
    for g in range(ngroups):
        for i in range(rounds):
            alone = [plan[p][1][i][0] & (plan[p][1][i][0] - 1) == 0 for p in range(parts)]
            if all(alone):
                when = own_at[g] + group_time[g] * (plan[0][1][i][1] + 1) / rounds
            else:
                lead = group_time[g] * (rounds - 1 - i) / rounds
                when = rel_at[g] - lead

            def arrival(g=g, i=i):
                for p in range(parts):
                    mask, step = plan[p][1][i]
                    wwait(mask, g, p, pr_sem.at[p, mask // 2, g])
                    for later in range(step + 1, steps):
                        wsend(mask, g, p, later)
                    csend(mask, g, p)
                if i == 0 and g + 2 < ngroups:
                    own_sends(g + 2)

            timed.append((when, 0, len(timed), arrival))
            events["w", g, i] = when
    for h in range(M - 1):
        for c in range(xchunks):
            when = (h + (c + 1) / xchunks) * shard_time

            def xarrival(h=h, c=c):
                xwait(h, c)
                if h + 1 < M - 1:
                    xstart(h + 1, c)

            timed.append((when, 1, len(timed), xarrival))
            events["x", h, c] = when
    xdone = (M - 1) * shard_time
    events["start"] = 0.0

    core_waited = set()

    def partner(g, masks):
        for mask in masks:
            for p in range(parts):
                if (g, mask, p) not in core_waited:
                    core_waited.add((g, mask, p))
                    wwait(mask + 1, g, p, cr_sem.at[p, mask // 2, g])

    begun = set()

    def unit(shard, g, masks):
        partner(g, masks)
        lo, n = spans[g]
        part = jnp.dot(x_n[shard], w_bufs[g][shard], preferred_element_type=F32)
        if g in begun:
            acc[:, lo:lo + n] += part
        else:
            acc[:, lo:lo + n] = part
            begun.add(g)

    evens = list(range(0, D, 2))

    def gained(r):
        if r == 0:
            xown.wait()
        shard = flip(m, r)
        block = 32

        @pl.loop(0, rows // block)
        def _(i):
            rr = pl.ds(pl.multiple_of(i * block, block), block)
            xv = x_all[shard, rr, :].astype(F32)
            ss[rr, :] += jnp.sum(xv * xv, axis=1, keepdims=True)
            x_n[shard, rr, :] = (xv * gain_s[shard]).astype(BF16)

    def inverse_rms():
        ss[...] = lax.rsqrt(ss[...] / model_width + 1e-05)

    def rope(x, cos, sin):
        turned = jnp.concatenate([x[:, half:], x[:, :half]], axis=1)
        return (x * cos + turned * sin).astype(BF16)

    def scores_of(q, k):
        return lax.dot_general(
            q, k, (((1,), (1,)), ((), ())), preferred_element_type=F32
        ) / math.sqrt(HEAD_SIZE)

    def softmax(logits):
        e = jnp.exp(logits - jnp.max(logits, axis=1, keepdims=True))
        return (e * (1.0 / jnp.sum(e, axis=1, keepdims=True))).astype(BF16)

    def first_exchange():
        for cp in early:
            cp.wait()
        arrive(dir_all, r2, D)
        direction = dir_all[0]
        for j in range(1, D):
            direction = direction + dir_all[j]
        weighted = fgain_ref[...].astype(F32).reshape(1, width) * direction
        toks = [tail_tok[b].astype(F32)[15:16, :] for b in range(S)]
        tok = toks[0] if S == 1 else jnp.concatenate(toks, axis=0)
        for jj in range(R):
            g_src[jj, 0:S, :] = weighted[:, jj * cols:(jj + 1) * cols]
            g_src[jj, S:2 * S, :] = tok[:, jj * cols:(jj + 1) * cols]
        for i in range(M - 1, -1, -1):
            k = (m + i) % M
            for jj in range(R):
                to = m * R + jj
                if i == 0:
                    remote(g_src.at[jj], g_all.at[d], s6.at[jj, i], r6.at[d], (to, k), to != d)
                    local(g_src.at[jj], g_all.at[d], r6.at[d], to == d)
                else:
                    remote(g_src.at[jj], g_all.at[d], s6.at[jj, i], r6.at[d], (to, k))

    def stacked(which):
        got = [g_all[j][which * S:(which + 1) * S, :] for j in range(D)]
        return jnp.concatenate(got, axis=0)

    def last_queries():
        arrive(g_all, r6, D)
        block = pl.ds(pl.multiple_of((d % R) * cols, cols), cols)
        lhs = (stacked(1) * gain_s[home, :, block]).astype(BF16)
        mine = pl.ds((d % R) * depth, depth)
        for g in range(1, ngroups):
            lo, n = spans[g]
            for p in range(parts):
                own_ready(g, p)
            part = jnp.dot(lhs, w_bufs[g][home, mine, :], preferred_element_type=F32)
            for j in range(D):
                qp_src[j, :, lo:lo + n] = part[j * S:(j + 1) * S, :]
        spread(qp_src, qp_all, s8, r8)

    def turned_back(x):
        return lax.dot_general(
            x, wout_ref[...], (((1,), (1,)), ((), ())), preferred_element_type=F32
        )

    def early_grads():
        exact = stacked(0)
        coarse = exact.astype(BF16)
        fine = (exact - coarse.astype(F32)).astype(BF16)
        pre = turned_back(jnp.concatenate([coarse, fine, stacked(1).astype(BF16)], axis=0))
        pre_w[...] = pre[:DS] + pre[DS:2 * DS]
        pre_t[...] = pre[2 * DS:]

    def keys_values():
        for b in range(S):
            sb = slice(b * L, (b + 1) * L)
            for n in range(kv_heads):
                lo = qw + n * HEAD_SIZE
                inv = ss[sb, :]
                k_s[b * kv_heads + n] = rope(acc[sb, lo:lo + HEAD_SIZE] * inv, cos_ref[...], sin_ref[...])
                v_s[b * kv_heads + n] = (acc[sb, lo + kw:lo + kw + HEAD_SIZE] * inv).astype(BF16)

    def last_position():
        arrive(qp_all, r8, D)
        q_sum = qp_all[0]
        for j in range(1, D):
            q_sum = q_sum + qp_all[j]
        for b in range(S):
            end = (b + 1) * L - 1
            inv = ss[end:end + 1, :]
            for n in range(kv_heads):
                for g in range(per_kv):
                    h = n * per_kv + g
                    q_s[g:g + 1, :] = q_sum[b:b + 1, h * HEAD_SIZE:(h + 1) * HEAD_SIZE] * inv
                q = rope(q_s[...], cos_ref[L - 1:L, :], sin_ref[L - 1:L, :])
                mixed = jnp.dot(
                    softmax(scores_of(q, k_s[b * kv_heads + n])), v_s[b * kv_heads + n],
                    preferred_element_type=F32,
                ).astype(BF16).astype(F32)
                for g in range(per_kv):
                    h = n * per_kv + g
                    last_src[b:b + 1, h * HEAD_SIZE:(h + 1) * HEAD_SIZE] = mixed[g:g + 1, :]
        spread(last_src, last_all, s1, r1, same=True)

    def project_out():
        arrive(last_all, r1, D)
        for j in range(D):
            rows_a[j * S:(j + 1) * S, :] = last_all[j]
        out_src[...] = jnp.dot(
            rows_a[...].astype(BF16), wout_ref[...], preferred_element_type=F32
        )
        for i in range(1, M):
            to = (m + i) % M
            remote(out_src, out_all.at[m], s3.at[i], r3.at[m], (d, to))
        local(out_src, out_all.at[m], r3.at[m])

    def residual_grads():
        arrive(out_all, r3, M)
        total = out_all[0]
        for k in range(1, M):
            total = total + out_all[k]
        attn = total.astype(BF16)
        residual = stacked(1) + attn.astype(F32)
        sq = jnp.sum(residual * residual, axis=1, keepdims=True)
        prod = jnp.sum(residual * stacked(0), axis=1, keepdims=True)
        back = turned_back(attn) + pre_t[...]
        entries = back.shape[1]
        sq = jnp.broadcast_to(sq, (DS, entries))
        prod = jnp.broadcast_to(prod, (DS, entries))
        ahead = pre_w[...]
        for j in range(D):
            sj = slice(j * S, (j + 1) * S)
            hg_src[j, 0:S, :] = ahead[sj]
            hg_src[j, S:2 * S, :] = back[sj]
            hg_src[j, 2 * S:3 * S, :] = sq[sj]
            hg_src[j, 3 * S:4 * S, :] = prod[sj]
        spread(hg_src, hg_all, s7, r7)

    bands = 2
    band = L // bands
    below = (lax.broadcasted_iota(jnp.int32, (band, band), 0)
             >= lax.broadcasted_iota(jnp.int32, (band, band), 1))

    def attend(h):
        at = slice(h * HEAD_SIZE, (h + 1) * HEAD_SIZE)
        for b in range(S):
            n = b * kv_heads + h // per_kv
            sb = slice(b * L, (b + 1) * L)
            q = rope(acc[sb, at] * ss[sb, :], cos_ref[...], sin_ref[...])
            column = None
            for i in range(bands):
                lo, hi = i * band, (i + 1) * band
                logits = scores_of(q[lo:hi], k_s[n, 0:hi, :])
                diag = jnp.where(below, logits[:, lo:hi], -1e30)
                logits = diag if i == 0 else jnp.concatenate([logits[:, :lo], diag], axis=1)
                mixed = jnp.dot(
                    softmax(logits), v_s[n, 0:hi, :], preferred_element_type=F32
                ).astype(BF16)
                head_ref[b * L + lo:b * L + hi, at] = mixed
                part = jnp.sum(mixed.astype(F32), axis=0, keepdims=True)
                column = part if column is None else column + part
            if b == 0:
                tot_src[:, at] = column
            else:
                tot_src[:, at] += column

    def totals():
        spread(tot_src, tot_all, s4, r4, same=True)

    def finish():
        arrive(hg_all, r7, D)
        joint = hg_all[0]
        for j in range(1, D):
            joint = joint + hg_all[j]
        inverse = lax.rsqrt(joint[2 * S:3 * S, :] / model_width + 1e-05)
        metric = inverse * joint[3 * S:4 * S, :]
        metric_ref[...] = metric[:, 0:1]
        fall = metric * inverse * inverse / model_width
        grads = joint[0:S] * inverse - joint[S:2 * S] * fall
        arrive(tot_all, r4, D)
        mean = tot_all[0]
        for j in range(1, D):
            mean = mean + tot_all[j]
        mean = mean / token_count
        gap = (mean - last_src[...]) * grads
        lane = lax.broadcasted_iota(jnp.int32, (S, heads), 1)
        scores = jnp.zeros((S, heads), F32)
        for h in range(heads):
            part = jnp.sum(gap[:, h * HEAD_SIZE:(h + 1) * HEAD_SIZE], axis=1, keepdims=True)
            scores = jnp.where(lane == h, part, scores)
        scores_ref[...] = scores

    tasks = {}
    for r in range(M):
        deps = [("start", 2.0)] if r == 0 else [(("x", r - 1, xchunks - 1), 0.1)]
        tasks["gain", r] = (deps, 1.0, 0, functools.partial(gained, r))
    gains = [(("gain", r), 0.0) for r in range(M)]
    tasks["inv"] = (gains, 0.1, 0, inverse_rms)
    unit_names = {g: [] for g in range(ngroups)}
    for g in range(ngroups):
        cost = 0.25 * spans[g][1] / 128
        late = rel_at[g] > xdone
        for r in range(M):
            if late:
                masks = [k for k in range(D) if k // R == r and k % 2 == 0]
                deps = gains + [
                    (("w", g, i), 1.6) for i in range(rounds)
                    if i == 0 or any(plan[p][1][i][0] in masks for p in range(parts))
                ]
                fn = functools.partial(lambda g, r, ms: unit(flip(home, r), g, ms), g, r, masks)
            else:
                deps = [(("gain", r), 0.0)] + [(("w", g, i), 1.6) for i in range(rounds)]
                fn = functools.partial(lambda g, r: unit(flip(m, r), g, evens), g, r)
            tasks["unit", g, r] = (deps, cost, 1 if g == 0 else 4, fn)
            unit_names[g].append((("unit", g, r), 0.0))
    tasks["kv"] = (unit_names[0] + [("inv", 0.0)], 1.0, 1, keys_values)
    tasks["E2"] = ([("start", 5.0)], 0.5, 2, first_exchange)
    tasks["E3"] = ([("E2", 26.0)], 1.0, 2, last_queries)
    tasks["pre"] = ([("E3", 0.0)], 1.0, 5, early_grads)
    tasks["last"] = ([("kv", 0.0), ("E3", 20.0)], 1.5, 1, last_position)
    tasks["T1"] = ([("last", 8.0)], 1.0, 1, project_out)
    tasks["T2"] = ([("T1", 4.0), ("pre", 0.0)], 1.5, 1, residual_grads)
    for g in range(1, ngroups):
        for h in range(*head_span[g]):
            tasks["att", h] = ([("kv", 0.0)] + unit_names[g], 1.2, 6, functools.partial(attend, h))
    tasks["tot"] = ([(("att", h), 0.0) for h in range(heads)], 0.1, 7, totals)
    tasks["fin"] = ([("tot", 0.0), ("T2", 0.0)], 0.1, 8, finish)

    spread(contrib_ref, dir_all, s2, r2)
    for c in range(xchunks):
        xstart(0, c)
    own_sends(0)
    if ngroups > 1:
        own_sends(1)
    ordered = order_tasks(events, tasks)
    timed += [(when, 2, len(timed) + i, fn) for i, (when, fn) in enumerate(ordered)]
    for _, _, _, fn in sorted(timed, key=lambda t: t[:3]):
        fn()
    for g in range(ngroups):
        partner(g, evens)
    for h in range(M - 1):
        for c in range(xchunks):
            for side in range(2):
                @pl.when(xpred(h, side))
                def _(h=h, c=c, side=side):
                    xsend(h, c, side).wait_send()
    for cp, cond in pending:
        if cond is None:
            cp.wait_send()
        else:
            pl.when(cond)(cp.wait_send)


def tables():
    half = HEAD_SIZE // 2
    inv_freq = np.exp(np.arange(half) * (-2.0 * math.log(500000.0) / HEAD_SIZE))
    angles = np.arange(SEQUENCE_LENGTH)[:, None] * inv_freq[None, :]
    c, s = np.cos(angles), np.sin(angles)
    cos = np.concatenate([c, c], axis=1).astype(np.float32)
    return cos, np.concatenate([-s, s], axis=1).astype(np.float32)


def whole(D, M, tokens, gain, wq, wk, wv, w_out, contrib, final_gain):
    rows, width = tokens.shape
    S = rows // SEQUENCE_LENGTH
    depth = wq.shape[0]
    entries, cols = w_out.shape
    kvw = wk.shape[1] + wv.shape[1]
    total = wq.shape[1] + kvw
    heads, kv_heads = wq.shape[1] // HEAD_SIZE, wk.shape[1] // HEAD_SIZE
    parts = len(spread_plan(D))
    steps = len(spread_plan(D)[0][0])
    sizes = head_groups(heads, depth // parts)
    ngroups = len(sizes) + 1
    xchunks = 2
    half = D // 2
    R = D // M
    cos, sin = tables()
    DMA = pltpu.SemaphoreType.DMA
    ANY = pl.BlockSpec(memory_space=pl.ANY)
    V = pl.BlockSpec(memory_space=pltpu.VMEM)

    def f(*shape):
        return pltpu.VMEM(shape, F32)

    def h(*shape):
        return pltpu.VMEM(shape, BF16)

    return pl.pallas_call(
        functools.partial(whole_kernel, D, M, sizes, xchunks, rows * D),
        name="whole",
        out_shape=[
            jax.ShapeDtypeStruct((rows, entries), BF16),
            jax.ShapeDtypeStruct((S, heads), F32),
            jax.ShapeDtypeStruct((S, 1), F32),
        ],
        in_specs=[ANY, V, ANY, ANY, ANY, ANY, ANY, ANY, V, V],
        out_specs=[V, V, V],
        scratch_shapes=[h(M, width, n) for n in [kvw] + [k * HEAD_SIZE for k in sizes]] + [
            h(M, rows, width), h(M, rows, width), f(rows, total), f(M, 1, width), f(rows, 1),
            f(SEQUENCE_LENGTH, HEAD_SIZE), f(SEQUENCE_LENGTH, HEAD_SIZE),
            h(entries, cols), h(S, 16, width), f(heads // kv_heads, HEAD_SIZE),
            h(S * kv_heads, SEQUENCE_LENGTH, HEAD_SIZE), h(S * kv_heads, SEQUENCE_LENGTH, HEAD_SIZE),
            f(D, S, width), f(R, 2 * S, cols), f(D, 2 * S, cols),
            f(D, S, entries), f(D, S, entries), f(D * S, entries), f(D * S, entries),
            f(S, entries), f(D, S, entries), f(D * S, entries),
            f(D * S, cols), f(M, D * S, cols), f(D, 4 * S, entries), f(D, 4 * S, entries),
            f(1, entries), f(D, 1, entries),
            DMA((ngroups, parts, 2)), DMA((4 + S,)),
            DMA((M - 1, xchunks, 2)), DMA((M - 1, xchunks, 2)),
            DMA((parts, half, ngroups, steps)), DMA((parts, half, ngroups)),
            DMA((parts, half, ngroups)), DMA((parts, half, ngroups)),
            DMA((D,)), DMA((D,)), DMA((D,)), DMA((D,)), DMA((M,)), DMA((M,)), DMA((D,)), DMA((D,)),
            DMA((R, M)), DMA((D,)), DMA((D,)), DMA((D,)), DMA((D,)), DMA((D,)),
        ],
        compiler_params=pltpu.CompilerParams(
            collective_id=0, has_side_effects=True, vmem_limit_bytes=56 * 1024 * 1024
        ),
    )(tokens, gain, wq, wk, wv, jnp.asarray(cos), jnp.asarray(sin), w_out, contrib,
      final_gain)


GROUP = 16


def pick_kernel(per, vocab_rows, clean_ref, corrupt_ref, *refs):
    blocks, out_ref = refs[:-1], refs[-1]
    step = pl.program_id(0)
    start = lax.axis_index("dp") * vocab_rows
    where = lax.broadcasted_iota(jnp.int32, (GROUP, 1), 0)
    for i in range(per):
        rows = []
        for side in range(2):
            at = (clean_ref, corrupt_ref)[side][step * per + i] - start
            block = blocks[side * per + i][...].astype(F32)
            hit = (where == at % GROUP) & (at >= 0) & (at < vocab_rows)
            rows.append(jnp.sum(jnp.where(hit, block, 0.0), axis=0, keepdims=True))
        out_ref[i] = rows[0] - rows[1]


def pick(unembed, clean_ids, corrupt_ids):
    vocab_rows, width = unembed.shape
    n = clean_ids.shape[0]
    per = min(8, n)

    def spec(side, i):
        def index(step, *ids):
            at = ids[side][step * per + i] - lax.axis_index("dp") * vocab_rows
            return jnp.clip(at, 0, vocab_rows - 1) // GROUP, 0
        return pl.BlockSpec((GROUP, width), index)

    return pl.pallas_call(
        functools.partial(pick_kernel, per, vocab_rows),
        name="pick",
        grid_spec=pltpu.PrefetchScalarGridSpec(
            num_scalar_prefetch=2,
            grid=(n // per,),
            in_specs=[spec(side, i) for side in range(2) for i in range(per)],
            out_specs=pl.BlockSpec((per, 1, width), lambda step, *ids: (step, 0, 0)),
        ),
        out_shape=jax.ShapeDtypeStruct((n, 1, width), F32),
    )(clean_ids, corrupt_ids, *([unembed] * (2 * per)))


def per_device(
    D, M, tokens, attn_gain, w_query, key_w, value_w, w_out, final_gain, unembed,
    clean_ids, corrupt_ids,
):
    S = tokens.shape[0] // SEQUENCE_LENGTH
    width = unembed.shape[1]
    contrib = pick(unembed, clean_ids, corrupt_ids).reshape(D, S, width)
    head_out, scores, metric = whole(
        D, M, tokens, attn_gain, w_query, key_w, value_w, w_out, contrib, final_gain
    )
    return head_out, scores, metric.reshape(S)


def solution(mesh):
    in_specs = (
        P("dp", "mp"), P(), P("dp", "mp"), P("dp", "mp"), P("dp", "mp"),
        P("mp", "dp"), P("mp"), P("dp", "mp"), P(), P(),
    )
    out_specs = (P("dp", "mp"), P("dp", "mp"), P("dp"))
    return jax.shard_map(
        functools.partial(per_device, mesh.shape["dp"], mesh.shape["mp"]),
        mesh=mesh, in_specs=in_specs, out_specs=out_specs, check_vma=False,
    )
```

```python
import functools
import math

import jax
import jax.numpy as jnp
import numpy as np
from jax import lax
from jax.experimental import pallas as pl
from jax.experimental.pallas import tpu as pltpu
from jax.sharding import PartitionSpec as P

HEAD_SIZE = 128
SEQUENCE_LENGTH = 256
MESH = pl.DeviceIdType.MESH
F32 = jnp.float32
BF16 = jnp.bfloat16
GROUP = 16


def flip(index, mask):
    bit = 1
    out = index
    while bit <= mask:
        if mask & bit:
            out = out + bit - 2 * bit * ((index // bit) % 2)
        bit *= 2
    return out


def spread_plan(size):
    bits = []
    bit = 2
    while bit < size:
        bits.append(bit)
        bit *= 2
    parts = min(2, len(bits))
    plan = []
    for part in range(parts):
        order = bits[part:] + bits[:part]
        held = [0]
        arrivals = []
        for step, b in enumerate(order):
            fresh = [h ^ b for h in held]
            arrivals += [(f, step) for f in fresh]
            held = held + fresh
        plan.append((order, arrivals))
    return plan


def head_groups(heads, piece):
    if piece < 256 or heads < 4:
        return [heads]
    sizes = [2] * ((heads - 2) // 2)
    return sizes + [1] * (heads - sum(sizes))


def order_tasks(events, tasks):
    done = dict(events)
    left = dict(tasks)
    clock = 0.0
    out = []
    while left:
        ready = {
            name: max([0.0] + [done[dep] + lag for dep, lag in deps])
            for name, (deps, dur, rank, fn) in left.items()
            if all(dep in done for dep, lag in deps)
        }
        now = [name for name in ready if ready[name] <= clock]
        if not now:
            clock = min(ready.values())
            continue
        name = min(now, key=lambda n: (left[n][2], ready[n]))
        deps, dur, rank, fn = left.pop(name)
        out.append((clock, fn))
        clock += dur
        done[name] = clock
    return out


def whole_kernel(
    D, M, sizes, xchunks, token_count, vocab,
    tok_ref, gain_ref, wq_ref, wk_ref, wv_ref, cos_hbm, sin_hbm, wout_hbm, fgain_ref, *rest,
):
    if vocab:
        unembed_ref, clean_ref, corrupt_ref = rest[:3]
        head_ref, scores_ref, metric_ref, contrib_ref, slab_a, slab_b, slab_sem = rest[3:10]
        scratch = rest[10:]
    else:
        contrib_ref, head_ref, scores_ref, metric_ref = rest[:4]
        scratch = rest[4:]
    G_ = len(sizes) + 1
    w_bufs = scratch[:G_]
    (
        x_all, x_n, acc, gain_s, ss, cos_ref, sin_ref, wout_ref, tail_tok, q_s, k_s, v_s,
        dir_all, g_src, g_all, t_src, t_all, qp_src, qp_all, pre_w, pre_t, last_src, last_all, rows_a,
        out_src, out_all, hg_src, hg_all, tot_src, tot_all,
        loc_sem, one_sem, xs_sem, xr_sem, ps_sem, pr_sem, cs_sem, cr_sem,
        s1, r1, s2, r2, s3, r3, s4, r4, s6, r6, s7, r7, s8, r8, s9, r9,
    ) = scratch[G_:]
    d = lax.axis_index("dp")
    m = lax.axis_index("mp")
    plan = spread_plan(D)
    parts = len(plan)
    steps = len(plan[0][0])
    depth = wq_ref.shape[0]
    rows, width = tok_ref.shape
    qw, kw, vw = wq_ref.shape[1], wk_ref.shape[1], wv_ref.shape[1]
    piece = depth // parts
    xpiece = rows // xchunks
    L = SEQUENCE_LENGTH
    S = rows // L
    heads, kv_heads = qw // HEAD_SIZE, kw // HEAD_SIZE
    per_kv = heads // kv_heads
    cols = wout_ref.shape[1]
    R = D // M
    everyone = D * M
    me = d * M + m
    model_width = M * width
    home = d // R
    half = HEAD_SIZE // 2
    DS = D * S

    spans = [(qw, kw + vw)]
    head_span = [None]
    at = 0
    for n in sizes:
        spans.append((at * HEAD_SIZE, n * HEAD_SIZE))
        head_span.append((at, at + n))
        at += n
    ngroups = len(spans)

    def wref(owner, g, p):
        return w_bufs[g].at[owner // R, pl.ds((owner % R) * depth + p * piece, piece), :]

    own = {}
    for g in range(ngroups):
        for p in range(parts):
            rr = pl.ds(p * piece, piece)
            dst = wref(d, g, p)
            lo, n = spans[g]
            if g == 0:
                moves = [(wk_ref.at[rr, :], dst.at[:, pl.ds(0, kw)]),
                         (wv_ref.at[rr, :], dst.at[:, pl.ds(kw, vw)])]
            else:
                moves = [(wq_ref.at[rr, pl.ds(lo, n)], dst)]
            own[g, p] = [
                pltpu.make_async_copy(a, b, loc_sem.at[g, p, i]) for i, (a, b) in enumerate(moves)
            ]
            for cp in own[g, p]:
                cp.start()

    barrier = pltpu.get_barrier_semaphore()

    @pl.loop(1, everyone)
    def _(i):
        other = (me + i) % everyone
        pl.semaphore_signal(
            barrier, inc=1, device_id=(other // M, other % M), device_id_type=MESH
        )

    xown = pltpu.make_async_copy(tok_ref, x_all.at[m], one_sem.at[0])
    early = [
        pltpu.make_async_copy(cos_hbm, cos_ref, one_sem.at[1]),
        pltpu.make_async_copy(sin_hbm, sin_ref, one_sem.at[2]),
        pltpu.make_async_copy(wout_hbm, wout_ref, one_sem.at[3]),
    ]
    for b in range(S):
        early.append(pltpu.make_async_copy(
            tok_ref.at[pl.ds((b + 1) * L - 16, 16), :], tail_tok.at[b], one_sem.at[4 + b]
        ))
    for cp in early[3:] + early[:3]:
        cp.start()
    xown.start()
    for cp in early[3:]:
        cp.wait()
    toks = [tail_tok[b].astype(F32)[15:16, :] for b in range(S)]
    tok = toks[0] if S == 1 else jnp.concatenate(toks, axis=0)
    for jj in range(R):
        t_src[jj] = tok[:, jj * cols:(jj + 1) * cols]
    for k in range(M):
        gain_s[k] = gain_ref[k * width:(k + 1) * width].astype(F32).reshape(1, width)
    ss[...] = jnp.zeros_like(ss)
    pl.semaphore_wait(barrier, everyone - 1)

    pending = []

    def remote(src, dst, send_sem, recv_sem, to, cond=None):
        cp = pltpu.make_async_remote_copy(
            src_ref=src, dst_ref=dst, send_sem=send_sem, recv_sem=recv_sem,
            device_id=to, device_id_type=MESH,
        )
        if cond is None:
            cp.start()
        else:
            pl.when(cond)(cp.start)
        pending.append((cp, cond))

    def local(src, dst, sem, cond=None):
        cp = pltpu.make_async_copy(src, dst, sem)
        if cond is None:
            cp.start()
        else:
            pl.when(cond)(cp.start)

    def arrive(buf, sem, n):
        for i in range(n):
            pltpu.make_async_copy(buf.at[i], buf.at[i], sem.at[i]).wait()

    def spread(src, dst, send_sem, recv_sem, same=False):
        for i in range(1, D):
            to = (d + i) % D
            remote(src if same else src.at[to], dst.at[d], send_sem.at[i], recv_sem.at[d], (to, m))
        local(src if same else src.at[d], dst.at[d], recv_sem.at[d])

    def xsend(hop, c, side):
        rr = pl.ds(c * xpiece, xpiece)
        owner = m - hop if side == 0 else m + hop
        to = m + 1 if side == 0 else m - 1
        return pltpu.make_async_remote_copy(
            src_ref=(tok_ref.at[rr, :] if hop == 0 else x_all.at[owner, rr, :]),
            dst_ref=x_all.at[owner, rr, :],
            send_sem=xs_sem.at[hop, c, side],
            recv_sem=xr_sem.at[hop, c, side],
            device_id=(d, to),
            device_id_type=MESH,
        )

    def xpred(hop, side):
        if side == 0:
            return (m < M - 1) & (m - hop >= 0)
        return (m > 0) & (m + hop < M)

    def xstart(hop, c):
        for side in range(2):
            @pl.when(xpred(hop, side))
            def _(side=side):
                xsend(hop, c, side).start()

    def xwait(hop, c):
        rr = pl.ds(c * xpiece, xpiece)
        for side in range(2):
            owner = m - hop - 1 if side == 0 else m + hop + 1
            ok = (m - hop - 1 >= 0) if side == 0 else (m + hop + 1 < M)

            @pl.when(ok)
            def _(side=side, owner=owner):
                pltpu.make_async_copy(
                    x_all.at[owner, rr, :], x_all.at[owner, rr, :], xr_sem.at[hop, c, side]
                ).wait()

    def wcopy(mask, g, p, bit, send_sem, recv_sem):
        ref = wref(flip(d, mask), g, p)
        remote(ref, ref, send_sem, recv_sem, (flip(d, bit), m))

    def wsend(mask, g, p, step):
        bit = plan[p][0][step]
        wcopy(mask, g, p, bit, ps_sem.at[p, mask // 2, g, step],
              pr_sem.at[p, (mask ^ bit) // 2, g])

    def csend(mask, g, p):
        wcopy(mask, g, p, 1, cs_sem.at[p, mask // 2, g], cr_sem.at[p, mask // 2, g])

    def wwait(mask, g, p, sem):
        ref = wref(flip(d, mask), g, p)
        pltpu.make_async_copy(ref, ref, sem).wait()

    def own_ready(g, p):
        for cp in own.pop((g, p), []):
            cp.wait()

    def own_sends(g):
        for p in range(parts):
            own_ready(g, p)
            wsend(0, g, p, 0)
        for step in range(1, steps):
            for p in range(parts):
                wsend(0, g, p, step)
        for p in range(parts):
            csend(0, g, p)

    pace = 46e3
    hops = len(plan[0][0])
    rounds = len(plan[0][1])
    shard_time = rows * width * 2 / pace
    group_time = [(D // 2 - 1) * depth * n * 2 / hops / pace for _, n in spans]
    share = hops / rounds
    own_at, rel_at = {}, {}
    clock = 0.0
    queue = [("own", 0)] + ([("own", 1)] if ngroups > 1 else [])
    for g in range(ngroups):
        queue.append(("rel", g))
        if g + 2 < ngroups:
            queue.append(("own", g + 2))
    for kind, g in queue:
        if kind == "own":
            own_at[g] = clock
            clock += group_time[g] * share
        else:
            clock += group_time[g] * (1 - share)
            rel_at[g] = clock

    timed = []
    events = {}
    for g in range(ngroups):
        for i in range(rounds):
            alone = [plan[p][1][i][0] & (plan[p][1][i][0] - 1) == 0 for p in range(parts)]
            if all(alone):
                when = own_at[g] + group_time[g] * (plan[0][1][i][1] + 1) / rounds
            else:
                lead = group_time[g] * (rounds - 1 - i) / rounds
                when = rel_at[g] - lead

            def arrival(g=g, i=i):
                for p in range(parts):
                    mask, step = plan[p][1][i]
                    wwait(mask, g, p, pr_sem.at[p, mask // 2, g])
                    for later in range(step + 1, steps):
                        wsend(mask, g, p, later)
                    csend(mask, g, p)
                if i == 0 and g + 2 < ngroups:
                    own_sends(g + 2)

            timed.append((when, 0, len(timed), arrival))
            events["w", g, i] = when
    for h in range(M - 1):
        for c in range(xchunks):
            when = (h + (c + 1) / xchunks) * shard_time

            def xarrival(h=h, c=c):
                xwait(h, c)
                if h + 1 < M - 1:
                    xstart(h + 1, c)

            timed.append((when, 1, len(timed), xarrival))
            events["x", h, c] = when
    xdone = (M - 1) * shard_time
    events["start"] = 0.0

    core_waited = set()

    def partner(g, masks):
        for mask in masks:
            for p in range(parts):
                if (g, mask, p) not in core_waited:
                    core_waited.add((g, mask, p))
                    wwait(mask + 1, g, p, cr_sem.at[p, mask // 2, g])

    begun = set()

    def unit(shard, g, masks):
        partner(g, masks)
        lo, n = spans[g]
        part = jnp.dot(x_n[shard], w_bufs[g][shard], preferred_element_type=F32)
        if g in begun:
            acc[:, lo:lo + n] += part
        else:
            acc[:, lo:lo + n] = part
            begun.add(g)

    evens = list(range(0, D, 2))

    def gained(r):
        if r == 0:
            xown.wait()
        shard = flip(m, r)
        block = 32

        @pl.loop(0, rows // block)
        def _(i):
            rr = pl.ds(pl.multiple_of(i * block, block), block)
            xv = x_all[shard, rr, :].astype(F32)
            ss[rr, :] += jnp.sum(xv * xv, axis=1, keepdims=True)
            x_n[shard, rr, :] = (xv * gain_s[shard]).astype(BF16)

    def inverse_rms():
        ss[...] = lax.rsqrt(ss[...] / model_width + 1e-05)

    def rope(x, cos, sin):
        turned = jnp.concatenate([x[:, half:], x[:, :half]], axis=1)
        return (x * cos + turned * sin).astype(BF16)

    def scores_of(q, k):
        return lax.dot_general(
            q, k, (((1,), (1,)), ((), ())), preferred_element_type=F32
        ) / math.sqrt(HEAD_SIZE)

    def softmax(logits):
        e = jnp.exp(logits - jnp.max(logits, axis=1, keepdims=True))
        return (e * (1.0 / jnp.sum(e, axis=1, keepdims=True))).astype(BF16)

    def fan(src, dst, send_sem, recv_sem):
        for i in range(M - 1, -1, -1):
            k = (m + i) % M
            for jj in range(R):
                to = m * R + jj
                if i == 0:
                    remote(src.at[jj], dst.at[d], send_sem.at[jj, i], recv_sem.at[d], (to, k), to != d)
                    local(src.at[jj], dst.at[d], recv_sem.at[d], to == d)
                else:
                    remote(src.at[jj], dst.at[d], send_sem.at[jj, i], recv_sem.at[d], (to, k))

    slabs = []
    if vocab:
        size = -(-vocab // (4 * GROUP)) * GROUP
        for k, lo in enumerate(range(0, vocab, size)):
            n = min(size, vocab - lo)
            buf = (slab_a, slab_b)[k % 2]
            slabs.append((lo, n, buf, pltpu.make_async_copy(
                unembed_ref.at[pl.ds(lo // GROUP, n // GROUP)], buf.at[pl.ds(0, n // GROUP)],
                slab_sem.at[k],
            )))
    where = lax.broadcasted_iota(jnp.int32, (GROUP, 1), 0)

    def pick_rows(k):
        lo, n, buf, cp = slabs[k]
        cp.wait()
        for i in range(DS):
            picked = []
            for ids in (clean_ref, corrupt_ref):
                at = ids[i] - (d * vocab + lo)
                block = lax.div(jnp.minimum(jnp.maximum(at, 0), n - 1), GROUP)
                got = buf[block].astype(F32)
                hit = where == at - block * GROUP
                picked.append(jnp.sum(jnp.where(hit, got, 0.0), axis=0, keepdims=True))
            row = slice(i % S, i % S + 1)
            if k == 0:
                contrib_ref[i // S, row, :] = picked[0] - picked[1]
            else:
                contrib_ref[i // S, row, :] += picked[0] - picked[1]
        if k + 2 < len(slabs):
            slabs[k + 2][3].start()

    def send_rows():
        spread(contrib_ref, dir_all, s2, r2)

    def first_exchange():
        arrive(dir_all, r2, D)
        direction = dir_all[0]
        for j in range(1, D):
            direction = direction + dir_all[j]
        weighted = fgain_ref[...].astype(F32).reshape(1, width) * direction
        for jj in range(R):
            g_src[jj] = weighted[:, jj * cols:(jj + 1) * cols]
        fan(g_src, g_all, s6, r6)

    def joined(buf):
        return jnp.concatenate([buf[j] for j in range(D)], axis=0)

    def last_queries():
        for cp in early[:3]:
            cp.wait()
        arrive(t_all, r9, D)
        block = pl.ds(pl.multiple_of((d % R) * cols, cols), cols)
        lhs = (joined(t_all) * gain_s[home, :, block]).astype(BF16)
        mine = pl.ds((d % R) * depth, depth)
        for g in range(1, ngroups):
            lo, n = spans[g]
            for p in range(parts):
                own_ready(g, p)
            part = jnp.dot(lhs, w_bufs[g][home, mine, :], preferred_element_type=F32)
            for j in range(D):
                qp_src[j, :, lo:lo + n] = part[j * S:(j + 1) * S, :]
        spread(qp_src, qp_all, s8, r8)

    def turned_back(x):
        return lax.dot_general(
            x, wout_ref[...], (((1,), (1,)), ((), ())), preferred_element_type=F32
        )

    def early_grads():
        arrive(g_all, r6, D)
        exact = joined(g_all)
        coarse = exact.astype(BF16)
        fine = (exact - coarse.astype(F32)).astype(BF16)
        pre = turned_back(jnp.concatenate([coarse, fine, joined(t_all).astype(BF16)], axis=0))
        pre_w[...] = pre[:DS] + pre[DS:2 * DS]
        pre_t[...] = pre[2 * DS:]

    def keys_values():
        for b in range(S):
            sb = slice(b * L, (b + 1) * L)
            for n in range(kv_heads):
                lo = qw + n * HEAD_SIZE
                inv = ss[sb, :]
                k_s[b * kv_heads + n] = rope(acc[sb, lo:lo + HEAD_SIZE] * inv, cos_ref[...], sin_ref[...])
                v_s[b * kv_heads + n] = (acc[sb, lo + kw:lo + kw + HEAD_SIZE] * inv).astype(BF16)

    def last_position():
        arrive(qp_all, r8, D)
        q_sum = qp_all[0]
        for j in range(1, D):
            q_sum = q_sum + qp_all[j]
        for b in range(S):
            end = (b + 1) * L - 1
            inv = ss[end:end + 1, :]
            for n in range(kv_heads):
                for g in range(per_kv):
                    h = n * per_kv + g
                    q_s[g:g + 1, :] = q_sum[b:b + 1, h * HEAD_SIZE:(h + 1) * HEAD_SIZE] * inv
                q = rope(q_s[...], cos_ref[L - 1:L, :], sin_ref[L - 1:L, :])
                mixed = jnp.dot(
                    softmax(scores_of(q, k_s[b * kv_heads + n])), v_s[b * kv_heads + n],
                    preferred_element_type=F32,
                ).astype(BF16).astype(F32)
                for g in range(per_kv):
                    h = n * per_kv + g
                    last_src[b:b + 1, h * HEAD_SIZE:(h + 1) * HEAD_SIZE] = mixed[g:g + 1, :]
        spread(last_src, last_all, s1, r1, same=True)

    def project_out():
        arrive(last_all, r1, D)
        for j in range(D):
            rows_a[j * S:(j + 1) * S, :] = last_all[j]
        out_src[...] = jnp.dot(
            rows_a[...].astype(BF16), wout_ref[...], preferred_element_type=F32
        )
        for i in range(1, M):
            to = (m + i) % M
            remote(out_src, out_all.at[m], s3.at[i], r3.at[m], (d, to))
        local(out_src, out_all.at[m], r3.at[m])

    def residual_grads():
        arrive(out_all, r3, M)
        total = out_all[0]
        for k in range(1, M):
            total = total + out_all[k]
        attn = total.astype(BF16)
        residual = joined(t_all) + attn.astype(F32)
        sq = jnp.sum(residual * residual, axis=1, keepdims=True)
        prod = jnp.sum(residual * joined(g_all), axis=1, keepdims=True)
        back = turned_back(attn) + pre_t[...]
        entries = back.shape[1]
        sq = jnp.broadcast_to(sq, (DS, entries))
        prod = jnp.broadcast_to(prod, (DS, entries))
        ahead = pre_w[...]
        for j in range(D):
            sj = slice(j * S, (j + 1) * S)
            hg_src[j, 0:S, :] = ahead[sj]
            hg_src[j, S:2 * S, :] = back[sj]
            hg_src[j, 2 * S:3 * S, :] = sq[sj]
            hg_src[j, 3 * S:4 * S, :] = prod[sj]
        spread(hg_src, hg_all, s7, r7)

    bands = 2
    band = L // bands
    below = (lax.broadcasted_iota(jnp.int32, (band, band), 0)
             >= lax.broadcasted_iota(jnp.int32, (band, band), 1))

    def attend(h):
        at = slice(h * HEAD_SIZE, (h + 1) * HEAD_SIZE)
        for b in range(S):
            n = b * kv_heads + h // per_kv
            sb = slice(b * L, (b + 1) * L)
            q = rope(acc[sb, at] * ss[sb, :], cos_ref[...], sin_ref[...])
            column = None
            for i in range(bands):
                lo, hi = i * band, (i + 1) * band
                logits = scores_of(q[lo:hi], k_s[n, 0:hi, :])
                diag = jnp.where(below, logits[:, lo:hi], -1e30)
                logits = diag if i == 0 else jnp.concatenate([logits[:, :lo], diag], axis=1)
                mixed = jnp.dot(
                    softmax(logits), v_s[n, 0:hi, :], preferred_element_type=F32
                ).astype(BF16)
                head_ref[b * L + lo:b * L + hi, at] = mixed
                part = jnp.sum(mixed.astype(F32), axis=0, keepdims=True)
                column = part if column is None else column + part
            if b == 0:
                tot_src[:, at] = column
            else:
                tot_src[:, at] += column

    def totals():
        spread(tot_src, tot_all, s4, r4, same=True)

    def finish():
        arrive(hg_all, r7, D)
        joint = hg_all[0]
        for j in range(1, D):
            joint = joint + hg_all[j]
        inverse = lax.rsqrt(joint[2 * S:3 * S, :] / model_width + 1e-05)
        metric = inverse * joint[3 * S:4 * S, :]
        metric_ref[...] = metric[:, 0:1]
        fall = metric * inverse * inverse / model_width
        grads = joint[0:S] * inverse - joint[S:2 * S] * fall
        arrive(tot_all, r4, D)
        mean = tot_all[0]
        for j in range(1, D):
            mean = mean + tot_all[j]
        mean = mean / token_count
        gap = (mean - last_src[...]) * grads
        lane = lax.broadcasted_iota(jnp.int32, (S, heads), 1)
        scores = jnp.zeros((S, heads), F32)
        for h in range(heads):
            part = jnp.sum(gap[:, h * HEAD_SIZE:(h + 1) * HEAD_SIZE], axis=1, keepdims=True)
            scores = jnp.where(lane == h, part, scores)
        scores_ref[...] = scores

    tasks = {}
    for r in range(M):
        deps = [("start", 2.0)] if r == 0 else [(("x", r - 1, xchunks - 1), 0.1)]
        tasks["gain", r] = (deps, 1.0, 0, functools.partial(gained, r))
    gains = [(("gain", r), 0.0) for r in range(M)]
    tasks["inv"] = (gains, 0.1, 0, inverse_rms)
    unit_names = {g: [] for g in range(ngroups)}
    for g in range(ngroups):
        cost = 0.25 * spans[g][1] / 128
        late = rel_at[g] > xdone
        for r in range(M):
            if late:
                masks = [k for k in range(D) if k // R == r and k % 2 == 0]
                deps = gains + [
                    (("w", g, i), 1.6) for i in range(rounds)
                    if i == 0 or any(plan[p][1][i][0] in masks for p in range(parts))
                ]
                fn = functools.partial(lambda g, r, ms: unit(flip(home, r), g, ms), g, r, masks)
            else:
                deps = [(("gain", r), 0.0)] + [(("w", g, i), 1.6) for i in range(rounds)]
                fn = functools.partial(lambda g, r: unit(flip(m, r), g, evens), g, r)
            tasks["unit", g, r] = (deps, cost, 1 if g == 0 else 4, fn)
            unit_names[g].append((("unit", g, r), 0.0))
    tasks["kv"] = (unit_names[0] + [("inv", 0.0), ("E3", 0.0)], 1.0, 1, keys_values)
    before = "start"
    for k in range(len(slabs)):
        tasks["pick", k] = ([(before, 4.0)], 1.2, 2, functools.partial(pick_rows, k))
        before = ("pick", k)
    tasks["E1"] = ([(before, 0.0)], 0.1, 2, send_rows)
    tasks["E2"] = ([("E1", 22.0)], 0.5, 2, first_exchange)
    tasks["E3"] = ([("start", 6.0)], 1.0, 2, last_queries)
    tasks["pre"] = ([("E2", 25.0)], 1.0, 5, early_grads)
    tasks["last"] = ([("kv", 0.0), ("E3", 20.0)], 1.5, 1, last_position)
    tasks["T1"] = ([("last", 8.0)], 1.0, 1, project_out)
    tasks["T2"] = ([("T1", 4.0), ("pre", 0.0)], 1.5, 1, residual_grads)
    for g in range(1, ngroups):
        for h in range(*head_span[g]):
            tasks["att", h] = ([("kv", 0.0)] + unit_names[g], 1.2, 6, functools.partial(attend, h))
    tasks["tot"] = ([(("att", h), 0.0) for h in range(heads)], 0.1, 7, totals)
    tasks["fin"] = ([("tot", 0.0), ("T2", 0.0)], 0.1, 8, finish)

    fan(t_src, t_all, s9, r9)
    for c in range(xchunks):
        xstart(0, c)
    own_sends(0)
    if ngroups > 1:
        own_sends(1)
    for slab in slabs[:2]:
        slab[3].start()
    ordered = order_tasks(events, tasks)
    timed += [(when, 2, len(timed) + i, fn) for i, (when, fn) in enumerate(ordered)]
    for _, _, _, fn in sorted(timed, key=lambda t: t[:3]):
        fn()
    for g in range(ngroups):
        partner(g, evens)
    for h in range(M - 1):
        for c in range(xchunks):
            for side in range(2):
                @pl.when(xpred(h, side))
                def _(h=h, c=c, side=side):
                    xsend(h, c, side).wait_send()
    for cp, cond in pending:
        if cond is None:
            cp.wait_send()
        else:
            pl.when(cond)(cp.wait_send)


def tables():
    half = HEAD_SIZE // 2
    inv_freq = np.exp(np.arange(half) * (-2.0 * math.log(500000.0) / HEAD_SIZE))
    angles = np.arange(SEQUENCE_LENGTH)[:, None] * inv_freq[None, :]
    c, s = np.cos(angles), np.sin(angles)
    cos = np.concatenate([c, c], axis=1).astype(np.float32)
    return cos, np.concatenate([-s, s], axis=1).astype(np.float32)


def whole(D, M, tokens, gain, wq, wk, wv, w_out, final_gain, unembed, clean_ids, corrupt_ids):
    rows, width = tokens.shape
    S = rows // SEQUENCE_LENGTH
    depth = wq.shape[0]
    entries, cols = w_out.shape
    kvw = wk.shape[1] + wv.shape[1]
    total = wq.shape[1] + kvw
    heads, kv_heads = wq.shape[1] // HEAD_SIZE, wk.shape[1] // HEAD_SIZE
    parts = len(spread_plan(D))
    steps = len(spread_plan(D)[0][0])
    sizes = head_groups(heads, depth // parts)
    ngroups = len(sizes) + 1
    xchunks = 2
    half = D // 2
    R = D // M
    cos, sin = tables()
    DMA = pltpu.SemaphoreType.DMA
    ANY = pl.BlockSpec(memory_space=pl.ANY)
    V = pl.BlockSpec(memory_space=pltpu.VMEM)

    def f(*shape):
        return pltpu.VMEM(shape, F32)

    def h(*shape):
        return pltpu.VMEM(shape, BF16)

    I = pl.BlockSpec(memory_space=pltpu.SMEM)
    vocab = unembed.shape[0] if unembed.shape[0] % GROUP == 0 else 0
    if vocab:
        slab = -(-vocab // (4 * GROUP)) * GROUP
        blocks = unembed.reshape(vocab // GROUP, GROUP, width)
        source, source_specs = (blocks, clean_ids, corrupt_ids), [ANY, I, I]
        pages = [h(slab // GROUP, GROUP, width)] * 2
        source_scratch = [f(D, S, width)] + pages + [DMA((4,))]
    else:
        source = (pick(unembed, clean_ids, corrupt_ids).reshape(D, S, width),)
        source_specs, source_scratch = [V], []
    return pl.pallas_call(
        functools.partial(whole_kernel, D, M, sizes, xchunks, rows * D, vocab),
        name="whole",
        out_shape=[
            jax.ShapeDtypeStruct((rows, entries), BF16),
            jax.ShapeDtypeStruct((S, heads), F32),
            jax.ShapeDtypeStruct((S, 1), F32),
        ],
        in_specs=[ANY, V, ANY, ANY, ANY, ANY, ANY, ANY, V] + source_specs,
        out_specs=[V, V, V],
        scratch_shapes=source_scratch + [h(M, width, n) for n in [kvw] + [k * HEAD_SIZE for k in sizes]] + [
            h(M, rows, width), h(M, rows, width), f(rows, total), f(M, 1, width), f(rows, 1),
            f(SEQUENCE_LENGTH, HEAD_SIZE), f(SEQUENCE_LENGTH, HEAD_SIZE),
            h(entries, cols), h(S, 16, width), f(heads // kv_heads, HEAD_SIZE),
            h(S * kv_heads, SEQUENCE_LENGTH, HEAD_SIZE), h(S * kv_heads, SEQUENCE_LENGTH, HEAD_SIZE),
            f(D, S, width), f(R, S, cols), f(D, S, cols), f(R, S, cols), f(D, S, cols),
            f(D, S, entries), f(D, S, entries), f(D * S, entries), f(D * S, entries),
            f(S, entries), f(D, S, entries), f(D * S, entries),
            f(D * S, cols), f(M, D * S, cols), f(D, 4 * S, entries), f(D, 4 * S, entries),
            f(1, entries), f(D, 1, entries),
            DMA((ngroups, parts, 2)), DMA((4 + S,)),
            DMA((M - 1, xchunks, 2)), DMA((M - 1, xchunks, 2)),
            DMA((parts, half, ngroups, steps)), DMA((parts, half, ngroups)),
            DMA((parts, half, ngroups)), DMA((parts, half, ngroups)),
            DMA((D,)), DMA((D,)), DMA((D,)), DMA((D,)), DMA((M,)), DMA((M,)), DMA((D,)), DMA((D,)),
            DMA((R, M)), DMA((D,)), DMA((D,)), DMA((D,)), DMA((D,)), DMA((D,)), DMA((R, M)), DMA((D,)),
        ],
        compiler_params=pltpu.CompilerParams(
            collective_id=0, has_side_effects=True, vmem_limit_bytes=56 * 1024 * 1024
        ),
    )(tokens, gain, wq, wk, wv, jnp.asarray(cos), jnp.asarray(sin), w_out,
      final_gain, *source)


def pick_kernel(per, vocab_rows, clean_ref, corrupt_ref, *refs):
    blocks, out_ref = refs[:-1], refs[-1]
    step = pl.program_id(0)
    start = lax.axis_index("dp") * vocab_rows
    where = lax.broadcasted_iota(jnp.int32, (GROUP, 1), 0)
    for i in range(per):
        rows = []
        for side in range(2):
            at = (clean_ref, corrupt_ref)[side][step * per + i] - start
            block = blocks[side * per + i][...].astype(F32)
            hit = (where == at % GROUP) & (at >= 0) & (at < vocab_rows)
            rows.append(jnp.sum(jnp.where(hit, block, 0.0), axis=0, keepdims=True))
        out_ref[i] = rows[0] - rows[1]


def pick(unembed, clean_ids, corrupt_ids):
    vocab_rows, width = unembed.shape
    n = clean_ids.shape[0]
    per = min(8, n)

    def spec(side, i):
        def index(step, *ids):
            at = ids[side][step * per + i] - lax.axis_index("dp") * vocab_rows
            return jnp.clip(at, 0, vocab_rows - 1) // GROUP, 0
        return pl.BlockSpec((GROUP, width), index)

    return pl.pallas_call(
        functools.partial(pick_kernel, per, vocab_rows),
        name="pick",
        grid_spec=pltpu.PrefetchScalarGridSpec(
            num_scalar_prefetch=2,
            grid=(n // per,),
            in_specs=[spec(side, i) for side in range(2) for i in range(per)],
            out_specs=pl.BlockSpec((per, 1, width), lambda step, *ids: (step, 0, 0)),
        ),
        out_shape=jax.ShapeDtypeStruct((n, 1, width), F32),
    )(clean_ids, corrupt_ids, *([unembed] * (2 * per)))


def per_device(
    D, M, tokens, attn_gain, w_query, key_w, value_w, w_out, final_gain, unembed,
    clean_ids, corrupt_ids,
):
    S = tokens.shape[0] // SEQUENCE_LENGTH
    head_out, scores, metric = whole(
        D, M, tokens, attn_gain, w_query, key_w, value_w, w_out, final_gain, unembed,
        clean_ids, corrupt_ids,
    )
    return head_out, scores, metric.reshape(S)


def solution(mesh):
    in_specs = (
        P("dp", "mp"), P(), P("dp", "mp"), P("dp", "mp"), P("dp", "mp"),
        P("mp", "dp"), P("mp"), P("dp", "mp"), P(), P(),
    )
    out_specs = (P("dp", "mp"), P("dp", "mp"), P("dp"))
    return jax.shard_map(
        functools.partial(per_device, mesh.shape["dp"], mesh.shape["mp"]),
        mesh=mesh, in_specs=in_specs, out_specs=out_specs, check_vma=False,
    )
```

```python
import functools
import math

import jax
import jax.numpy as jnp
import numpy as np
from jax import lax
from jax.experimental import pallas as pl
from jax.experimental.pallas import tpu as pltpu
from jax.sharding import PartitionSpec as P

HEAD_SIZE = 128
SEQUENCE_LENGTH = 256
MESH = pl.DeviceIdType.MESH
F32 = jnp.float32
BF16 = jnp.bfloat16
GROUP = 16


def flip(index, mask):
    bit = 1
    out = index
    while bit <= mask:
        if mask & bit:
            out = out + bit - 2 * bit * ((index // bit) % 2)
        bit *= 2
    return out


def spread_plan(size):
    bits = []
    bit = 2
    while bit < size:
        bits.append(bit)
        bit *= 2
    parts = min(2, len(bits))
    plan = []
    for part in range(parts):
        order = bits[part:] + bits[:part]
        held = [0]
        arrivals = []
        for step, b in enumerate(order):
            fresh = [h ^ b for h in held]
            arrivals += [(f, step) for f in fresh]
            held = held + fresh
        plan.append((order, arrivals))
    return plan


def head_groups(heads, piece):
    if piece < 256 or heads < 4:
        return [heads]
    sizes = [2] * ((heads - 4) // 2)
    return sizes + [1] * (heads - sum(sizes))


def order_tasks(events, tasks):
    done = dict(events)
    left = dict(tasks)
    clock = 0.0
    out = []
    while left:
        ready = {
            name: max([0.0] + [done[dep] + lag for dep, lag in deps])
            for name, (deps, dur, rank, fn) in left.items()
            if all(dep in done for dep, lag in deps)
        }
        now = [name for name in ready if ready[name] <= clock]
        if not now:
            clock = min(ready.values())
            continue
        name = min(now, key=lambda n: (left[n][2], ready[n]))
        deps, dur, rank, fn = left.pop(name)
        out.append((clock, fn))
        clock += dur
        done[name] = clock
    return out


def whole_kernel(
    D, M, sizes, xchunks, token_count, vocab,
    tok_ref, gain_ref, wq_ref, wk_ref, wv_ref, cos_hbm, sin_hbm, wout_hbm, fgain_ref, *rest,
):
    if vocab:
        unembed_ref, clean_ref, corrupt_ref = rest[:3]
        head_ref, scores_ref, metric_ref, contrib_ref, slab_a, slab_b, slab_sem = rest[3:10]
        scratch = rest[10:]
    else:
        contrib_ref, head_ref, scores_ref, metric_ref = rest[:4]
        scratch = rest[4:]
    G_ = len(sizes) + 1
    w_bufs = scratch[:G_]
    (
        x_all, x_n, acc, gain_s, ss, cos_ref, sin_ref, wout_ref, tail_tok, q_s, k_s, v_s,
        dir_all, g_src, g_all, t_src, t_all, qp_src, qp_all, pre_w, pre_t, last_src, last_all, rows_a,
        out_src, out_all, hg_src, hg_all, tot_src, tot_all,
        loc_sem, one_sem, xs_sem, xr_sem, ps_sem, pr_sem, cs_sem, cr_sem,
        s1, r1, s2, r2, s3, r3, s4, r4, s6, r6, s7, r7, s8, r8, s9, r9,
    ) = scratch[G_:]
    d = lax.axis_index("dp")
    m = lax.axis_index("mp")
    plan = spread_plan(D)
    parts = len(plan)
    steps = len(plan[0][0])
    depth = wq_ref.shape[0]
    rows, width = tok_ref.shape
    qw, kw, vw = wq_ref.shape[1], wk_ref.shape[1], wv_ref.shape[1]
    piece = depth // parts
    xpiece = rows // xchunks
    L = SEQUENCE_LENGTH
    S = rows // L
    heads, kv_heads = qw // HEAD_SIZE, kw // HEAD_SIZE
    per_kv = heads // kv_heads
    cols = wout_ref.shape[1]
    R = D // M
    everyone = D * M
    me = d * M + m
    model_width = M * width
    home = d // R
    half = HEAD_SIZE // 2
    DS = D * S

    spans = [(qw, kw + vw)]
    head_span = [None]
    at = 0
    for n in sizes:
        spans.append((at * HEAD_SIZE, n * HEAD_SIZE))
        head_span.append((at, at + n))
        at += n
    ngroups = len(spans)

    def wref(owner, g, p):
        return w_bufs[g].at[owner // R, pl.ds((owner % R) * depth + p * piece, piece), :]

    own = {}
    for g in range(ngroups):
        for p in range(parts):
            rr = pl.ds(p * piece, piece)
            dst = wref(d, g, p)
            lo, n = spans[g]
            if g == 0:
                moves = [(wk_ref.at[rr, :], dst.at[:, pl.ds(0, kw)]),
                         (wv_ref.at[rr, :], dst.at[:, pl.ds(kw, vw)])]
            else:
                moves = [(wq_ref.at[rr, pl.ds(lo, n)], dst)]
            own[g, p] = [
                pltpu.make_async_copy(a, b, loc_sem.at[g, p, i]) for i, (a, b) in enumerate(moves)
            ]
            for cp in own[g, p]:
                cp.start()

    barrier = pltpu.get_barrier_semaphore()

    @pl.loop(1, everyone)
    def _(i):
        other = (me + i) % everyone
        pl.semaphore_signal(
            barrier, inc=1, device_id=(other // M, other % M), device_id_type=MESH
        )

    xown = pltpu.make_async_copy(tok_ref, x_all.at[m], one_sem.at[0])
    early = [
        pltpu.make_async_copy(cos_hbm, cos_ref, one_sem.at[1]),
        pltpu.make_async_copy(sin_hbm, sin_ref, one_sem.at[2]),
        pltpu.make_async_copy(wout_hbm, wout_ref, one_sem.at[3]),
    ]
    for b in range(S):
        early.append(pltpu.make_async_copy(
            tok_ref.at[pl.ds((b + 1) * L - 16, 16), :], tail_tok.at[b], one_sem.at[4 + b]
        ))
    for cp in early[3:] + early[:3]:
        cp.start()
    xown.start()
    for cp in early[3:]:
        cp.wait()
    toks = [tail_tok[b].astype(F32)[15:16, :] for b in range(S)]
    tok = toks[0] if S == 1 else jnp.concatenate(toks, axis=0)
    for jj in range(R):
        t_src[jj] = tok[:, jj * cols:(jj + 1) * cols]
    for k in range(M):
        gain_s[k] = gain_ref[k * width:(k + 1) * width].astype(F32).reshape(1, width)
    ss[...] = jnp.zeros_like(ss)
    pl.semaphore_wait(barrier, everyone - 1)

    pending = []

    def remote(src, dst, send_sem, recv_sem, to, cond=None):
        cp = pltpu.make_async_remote_copy(
            src_ref=src, dst_ref=dst, send_sem=send_sem, recv_sem=recv_sem,
            device_id=to, device_id_type=MESH,
        )
        if cond is None:
            cp.start()
        else:
            pl.when(cond)(cp.start)
        pending.append((cp, cond))

    def local(src, dst, sem, cond=None):
        cp = pltpu.make_async_copy(src, dst, sem)
        if cond is None:
            cp.start()
        else:
            pl.when(cond)(cp.start)

    def arrive(buf, sem, n):
        for i in range(n):
            pltpu.make_async_copy(buf.at[i], buf.at[i], sem.at[i]).wait()

    def spread(src, dst, send_sem, recv_sem, same=False):
        for i in range(1, D):
            to = (d + i) % D
            remote(src if same else src.at[to], dst.at[d], send_sem.at[i], recv_sem.at[d], (to, m))
        local(src if same else src.at[d], dst.at[d], recv_sem.at[d])

    def xsend(hop, c, side):
        rr = pl.ds(c * xpiece, xpiece)
        owner = m - hop if side == 0 else m + hop
        to = m + 1 if side == 0 else m - 1
        return pltpu.make_async_remote_copy(
            src_ref=(tok_ref.at[rr, :] if hop == 0 else x_all.at[owner, rr, :]),
            dst_ref=x_all.at[owner, rr, :],
            send_sem=xs_sem.at[hop, c, side],
            recv_sem=xr_sem.at[hop, c, side],
            device_id=(d, to),
            device_id_type=MESH,
        )

    def xpred(hop, side):
        if side == 0:
            return (m < M - 1) & (m - hop >= 0)
        return (m > 0) & (m + hop < M)

    def xstart(hop, c):
        for side in range(2):
            @pl.when(xpred(hop, side))
            def _(side=side):
                xsend(hop, c, side).start()

    def xwait(hop, c):
        rr = pl.ds(c * xpiece, xpiece)
        for side in range(2):
            owner = m - hop - 1 if side == 0 else m + hop + 1
            ok = (m - hop - 1 >= 0) if side == 0 else (m + hop + 1 < M)

            @pl.when(ok)
            def _(side=side, owner=owner):
                pltpu.make_async_copy(
                    x_all.at[owner, rr, :], x_all.at[owner, rr, :], xr_sem.at[hop, c, side]
                ).wait()

    def wcopy(mask, g, p, bit, send_sem, recv_sem):
        ref = wref(flip(d, mask), g, p)
        remote(ref, ref, send_sem, recv_sem, (flip(d, bit), m))

    def wsend(mask, g, p, step):
        bit = plan[p][0][step]
        wcopy(mask, g, p, bit, ps_sem.at[p, mask // 2, g, step],
              pr_sem.at[p, (mask ^ bit) // 2, g])

    def csend(mask, g, p):
        wcopy(mask, g, p, 1, cs_sem.at[p, mask // 2, g], cr_sem.at[p, mask // 2, g])

    def wwait(mask, g, p, sem):
        ref = wref(flip(d, mask), g, p)
        pltpu.make_async_copy(ref, ref, sem).wait()

    def own_ready(g, p):
        for cp in own.pop((g, p), []):
            cp.wait()

    def own_send(g, step):
        for p in range(parts):
            own_ready(g, p)
            wsend(0, g, p, step)
        if step == steps - 1:
            for p in range(parts):
                csend(0, g, p)

    pace = 46e3
    hops = len(plan[0][0])
    rounds = len(plan[0][1])
    shard_time = rows * width * 2 / pace
    group_time = [(D // 2 - 1) * depth * n * 2 / hops / pace for _, n in spans]
    share = hops / rounds
    own_at, rel_at = {}, {}
    clock = 0.0
    queue = []
    for g in range(ngroups):
        queue += [("own", g), ("rel", g)]
    for kind, g in queue:
        if kind == "own":
            own_at[g] = clock
            clock += group_time[g] * share
        else:
            clock += group_time[g] * (1 - share)
            rel_at[g] = clock

    timed = []
    events = {}
    for g in range(ngroups):
        for i in range(rounds):
            alone = [plan[p][1][i][0] & (plan[p][1][i][0] - 1) == 0 for p in range(parts)]
            if all(alone):
                when = own_at[g] + group_time[g] * (plan[0][1][i][1] + 1) / rounds
            else:
                lead = group_time[g] * (rounds - 1 - i) / rounds
                when = rel_at[g] - lead

            def arrival(g=g, i=i):
                for p in range(parts):
                    mask, step = plan[p][1][i]
                    wwait(mask, g, p, pr_sem.at[p, mask // 2, g])
                    for later in range(step + 1, steps):
                        wsend(mask, g, p, later)
                    csend(mask, g, p)

            timed.append((when, 0, len(timed), arrival))
            events["w", g, i] = when
    for h in range(M - 1):
        for c in range(xchunks):
            when = (h + (c + 1) / xchunks) * shard_time

            def xarrival(h=h, c=c):
                xwait(h, c)
                if h + 1 < M - 1:
                    xstart(h + 1, c)

            timed.append((when, 1, len(timed), xarrival))
            events["x", h, c] = when
    xdone = (M - 1) * shard_time
    events["start"] = 0.0

    core_waited = set()

    def partner(g, masks):
        for mask in masks:
            for p in range(parts):
                if (g, mask, p) not in core_waited:
                    core_waited.add((g, mask, p))
                    wwait(mask + 1, g, p, cr_sem.at[p, mask // 2, g])

    begun = set()

    def unit(shard, g, masks):
        partner(g, masks)
        lo, n = spans[g]
        part = jnp.dot(x_n[shard], w_bufs[g][shard], preferred_element_type=F32)
        if g in begun:
            acc[:, lo:lo + n] += part
        else:
            acc[:, lo:lo + n] = part
            begun.add(g)

    evens = list(range(0, D, 2))

    def gained(r):
        if r == 0:
            xown.wait()
        shard = flip(m, r)
        block = 32

        @pl.loop(0, rows // block)
        def _(i):
            rr = pl.ds(pl.multiple_of(i * block, block), block)
            xv = x_all[shard, rr, :].astype(F32)
            ss[rr, :] += jnp.sum(xv * xv, axis=1, keepdims=True)
            x_n[shard, rr, :] = (xv * gain_s[shard]).astype(BF16)

    def inverse_rms():
        ss[...] = lax.rsqrt(ss[...] / model_width + 1e-05)

    def rope(x, cos, sin):
        turned = jnp.concatenate([x[:, half:], x[:, :half]], axis=1)
        return (x * cos + turned * sin).astype(BF16)

    def scores_of(q, k):
        return lax.dot_general(
            q, k, (((1,), (1,)), ((), ())), preferred_element_type=F32
        ) / math.sqrt(HEAD_SIZE)

    def softmax(logits):
        e = jnp.exp(logits - jnp.max(logits, axis=1, keepdims=True))
        return (e * (1.0 / jnp.sum(e, axis=1, keepdims=True))).astype(BF16)

    def fan(src, dst, send_sem, recv_sem):
        for i in range(M - 1, -1, -1):
            k = (m + i) % M
            for jj in range(R):
                to = m * R + jj
                if i == 0:
                    remote(src.at[jj], dst.at[d], send_sem.at[jj, i], recv_sem.at[d], (to, k), to != d)
                    local(src.at[jj], dst.at[d], recv_sem.at[d], to == d)
                else:
                    remote(src.at[jj], dst.at[d], send_sem.at[jj, i], recv_sem.at[d], (to, k))

    slabs = []
    if vocab:
        size = -(-vocab // (4 * GROUP)) * GROUP
        for k, lo in enumerate(range(0, vocab, size)):
            n = min(size, vocab - lo)
            buf = (slab_a, slab_b)[k % 2]
            slabs.append((lo, n, buf, pltpu.make_async_copy(
                unembed_ref.at[pl.ds(lo // GROUP, n // GROUP)], buf.at[pl.ds(0, n // GROUP)],
                slab_sem.at[k],
            )))
    where = lax.broadcasted_iota(jnp.int32, (GROUP, 1), 0)

    def pick_rows(k):
        lo, n, buf, cp = slabs[k]
        cp.wait()
        for i in range(DS):
            picked = []
            for ids in (clean_ref, corrupt_ref):
                at = ids[i] - (d * vocab + lo)
                block = lax.div(jnp.minimum(jnp.maximum(at, 0), n - 1), GROUP)
                got = buf[block].astype(F32)
                hit = where == at - block * GROUP
                picked.append(jnp.sum(jnp.where(hit, got, 0.0), axis=0, keepdims=True))
            row = slice(i % S, i % S + 1)
            if k == 0:
                contrib_ref[i // S, row, :] = picked[0] - picked[1]
            else:
                contrib_ref[i // S, row, :] += picked[0] - picked[1]
        if k + 2 < len(slabs):
            slabs[k + 2][3].start()

    def send_rows():
        spread(contrib_ref, dir_all, s2, r2)

    def first_exchange():
        arrive(dir_all, r2, D)
        direction = dir_all[0]
        for j in range(1, D):
            direction = direction + dir_all[j]
        weighted = fgain_ref[...].astype(F32).reshape(1, width) * direction
        for jj in range(R):
            g_src[jj] = weighted[:, jj * cols:(jj + 1) * cols]
        fan(g_src, g_all, s6, r6)

    def joined(buf):
        return jnp.concatenate([buf[j] for j in range(D)], axis=0)

    def last_queries():
        for cp in early[:3]:
            cp.wait()
        arrive(t_all, r9, D)
        block = pl.ds(pl.multiple_of((d % R) * cols, cols), cols)
        lhs = (joined(t_all) * gain_s[home, :, block]).astype(BF16)
        mine = pl.ds((d % R) * depth, depth)
        for g in range(1, ngroups):
            lo, n = spans[g]
            for p in range(parts):
                own_ready(g, p)
            part = jnp.dot(lhs, w_bufs[g][home, mine, :], preferred_element_type=F32)
            for j in range(D):
                qp_src[j, :, lo:lo + n] = part[j * S:(j + 1) * S, :]
        spread(qp_src, qp_all, s8, r8)

    def turned_back(x):
        return lax.dot_general(
            x, wout_ref[...], (((1,), (1,)), ((), ())), preferred_element_type=F32
        )

    def early_grads():
        arrive(g_all, r6, D)
        exact = joined(g_all)
        coarse = exact.astype(BF16)
        fine = (exact - coarse.astype(F32)).astype(BF16)
        pre = turned_back(jnp.concatenate([coarse, fine, joined(t_all).astype(BF16)], axis=0))
        pre_w[...] = pre[:DS] + pre[DS:2 * DS]
        pre_t[...] = pre[2 * DS:]

    def keys_values():
        for b in range(S):
            sb = slice(b * L, (b + 1) * L)
            for n in range(kv_heads):
                lo = qw + n * HEAD_SIZE
                inv = ss[sb, :]
                k_s[b * kv_heads + n] = rope(acc[sb, lo:lo + HEAD_SIZE] * inv, cos_ref[...], sin_ref[...])
                v_s[b * kv_heads + n] = (acc[sb, lo + kw:lo + kw + HEAD_SIZE] * inv).astype(BF16)

    def last_position():
        arrive(qp_all, r8, D)
        q_sum = qp_all[0]
        for j in range(1, D):
            q_sum = q_sum + qp_all[j]
        for b in range(S):
            end = (b + 1) * L - 1
            inv = ss[end:end + 1, :]
            for n in range(kv_heads):
                for g in range(per_kv):
                    h = n * per_kv + g
                    q_s[g:g + 1, :] = q_sum[b:b + 1, h * HEAD_SIZE:(h + 1) * HEAD_SIZE] * inv
                q = rope(q_s[...], cos_ref[L - 1:L, :], sin_ref[L - 1:L, :])
                mixed = jnp.dot(
                    softmax(scores_of(q, k_s[b * kv_heads + n])), v_s[b * kv_heads + n],
                    preferred_element_type=F32,
                ).astype(BF16).astype(F32)
                for g in range(per_kv):
                    h = n * per_kv + g
                    last_src[b:b + 1, h * HEAD_SIZE:(h + 1) * HEAD_SIZE] = mixed[g:g + 1, :]
        spread(last_src, last_all, s1, r1, same=True)

    def project_out():
        arrive(last_all, r1, D)
        for j in range(D):
            rows_a[j * S:(j + 1) * S, :] = last_all[j]
        out_src[...] = jnp.dot(
            rows_a[...].astype(BF16), wout_ref[...], preferred_element_type=F32
        )
        for i in range(1, M):
            to = (m + i) % M
            remote(out_src, out_all.at[m], s3.at[i], r3.at[m], (d, to))
        local(out_src, out_all.at[m], r3.at[m])

    def residual_grads():
        arrive(out_all, r3, M)
        total = out_all[0]
        for k in range(1, M):
            total = total + out_all[k]
        attn = total.astype(BF16)
        residual = joined(t_all) + attn.astype(F32)
        sq = jnp.sum(residual * residual, axis=1, keepdims=True)
        prod = jnp.sum(residual * joined(g_all), axis=1, keepdims=True)
        back = turned_back(attn) + pre_t[...]
        entries = back.shape[1]
        sq = jnp.broadcast_to(sq, (DS, entries))
        prod = jnp.broadcast_to(prod, (DS, entries))
        ahead = pre_w[...]
        for j in range(D):
            sj = slice(j * S, (j + 1) * S)
            hg_src[j, 0:S, :] = ahead[sj]
            hg_src[j, S:2 * S, :] = back[sj]
            hg_src[j, 2 * S:3 * S, :] = sq[sj]
            hg_src[j, 3 * S:4 * S, :] = prod[sj]
        spread(hg_src, hg_all, s7, r7)

    bands = 2
    band = L // bands
    below = (lax.broadcasted_iota(jnp.int32, (band, band), 0)
             >= lax.broadcasted_iota(jnp.int32, (band, band), 1))

    def attend(h):
        at = slice(h * HEAD_SIZE, (h + 1) * HEAD_SIZE)
        for b in range(S):
            n = b * kv_heads + h // per_kv
            sb = slice(b * L, (b + 1) * L)
            q = rope(acc[sb, at] * ss[sb, :], cos_ref[...], sin_ref[...])
            column = None
            for i in range(bands):
                lo, hi = i * band, (i + 1) * band
                logits = scores_of(q[lo:hi], k_s[n, 0:hi, :])
                diag = jnp.where(below, logits[:, lo:hi], -1e30)
                logits = diag if i == 0 else jnp.concatenate([logits[:, :lo], diag], axis=1)
                mixed = jnp.dot(
                    softmax(logits), v_s[n, 0:hi, :], preferred_element_type=F32
                ).astype(BF16)
                head_ref[b * L + lo:b * L + hi, at] = mixed
                part = jnp.sum(mixed.astype(F32), axis=0, keepdims=True)
                column = part if column is None else column + part
            if b == 0:
                tot_src[:, at] = column
            else:
                tot_src[:, at] += column

    def totals():
        spread(tot_src, tot_all, s4, r4, same=True)

    def finish():
        arrive(hg_all, r7, D)
        joint = hg_all[0]
        for j in range(1, D):
            joint = joint + hg_all[j]
        inverse = lax.rsqrt(joint[2 * S:3 * S, :] / model_width + 1e-05)
        metric = inverse * joint[3 * S:4 * S, :]
        metric_ref[...] = metric[:, 0:1]
        fall = metric * inverse * inverse / model_width
        grads = joint[0:S] * inverse - joint[S:2 * S] * fall
        arrive(tot_all, r4, D)
        mean = tot_all[0]
        for j in range(1, D):
            mean = mean + tot_all[j]
        mean = mean / token_count
        gap = (mean - last_src[...]) * grads
        lane = lax.broadcasted_iota(jnp.int32, (S, heads), 1)
        scores = jnp.zeros((S, heads), F32)
        for h in range(heads):
            part = jnp.sum(gap[:, h * HEAD_SIZE:(h + 1) * HEAD_SIZE], axis=1, keepdims=True)
            scores = jnp.where(lane == h, part, scores)
        scores_ref[...] = scores

    tasks = {}
    for r in range(M):
        deps = [("start", 2.0)] if r == 0 else [(("x", r - 1, xchunks - 1), 0.1)]
        tasks["gain", r] = (deps, 1.0, 0, functools.partial(gained, r))
    gains = [(("gain", r), 0.0) for r in range(M)]
    tasks["inv"] = (gains, 0.1, 0, inverse_rms)
    unit_names = {g: [] for g in range(ngroups)}
    for g in range(ngroups):
        cost = 0.25 * spans[g][1] / 128
        late = rel_at[g] > xdone
        for r in range(M):
            if late:
                masks = [k for k in range(D) if k // R == r and k % 2 == 0]
                deps = gains + [
                    (("w", g, i), 1.6) for i in range(rounds)
                    if i == 0 or any(plan[p][1][i][0] in masks for p in range(parts))
                ]
                fn = functools.partial(lambda g, r, ms: unit(flip(home, r), g, ms), g, r, masks)
            else:
                deps = [(("gain", r), 0.0)] + [(("w", g, i), 1.6) for i in range(rounds)]
                fn = functools.partial(lambda g, r: unit(flip(m, r), g, evens), g, r)
            tasks["unit", g, r] = (deps, cost, 1 if g == 0 else 4, fn)
            unit_names[g].append((("unit", g, r), 0.0))
    tasks["kv"] = (unit_names[0] + [("inv", 0.0), ("E3", 0.0)], 1.0, 1, keys_values)
    before = "start"
    for k in range(len(slabs)):
        tasks["pick", k] = ([(before, 4.0)], 1.2, 2, functools.partial(pick_rows, k))
        before = ("pick", k)
    tasks["E1"] = ([(before, 0.0)], 0.1, 2, send_rows)
    tasks["E2"] = ([("E1", 22.0)], 0.5, 2, first_exchange)
    tasks["E3"] = ([("start", 6.0)], 1.0, 2, last_queries)
    tasks["pre"] = ([("E2", 25.0)], 1.0, 5, early_grads)
    tasks["last"] = ([("kv", 0.0), ("E3", 20.0)], 1.5, 1, last_position)
    tasks["T1"] = ([("last", 8.0)], 1.0, 1, project_out)
    tasks["T2"] = ([("T1", 4.0), ("pre", 0.0)], 1.5, 1, residual_grads)
    for g in range(1, ngroups):
        for h in range(*head_span[g]):
            tasks["att", h] = ([("kv", 0.0)] + unit_names[g], 1.2, 6, functools.partial(attend, h))
    tasks["tot"] = ([(("att", h), 0.0) for h in range(heads)], 0.1, 7, totals)
    tasks["fin"] = ([("tot", 0.0), ("T2", 0.0)], 0.1, 8, finish)

    fan(t_src, t_all, s9, r9)
    for c in range(xchunks):
        xstart(0, c)
    for step in range(steps):
        own_send(0, step)
    for g in range(1, ngroups):
        for step in range(steps):
            when = own_at[g] + group_time[g] * share * step / steps - 4.0
            timed.append((when, -1, len(timed), functools.partial(own_send, g, step)))
    for slab in slabs[:2]:
        slab[3].start()
    ordered = order_tasks(events, tasks)
    timed += [(when, 2, len(timed) + i, fn) for i, (when, fn) in enumerate(ordered)]
    for _, _, _, fn in sorted(timed, key=lambda t: t[:3]):
        fn()
    for g in range(ngroups):
        partner(g, evens)
    for h in range(M - 1):
        for c in range(xchunks):
            for side in range(2):
                @pl.when(xpred(h, side))
                def _(h=h, c=c, side=side):
                    xsend(h, c, side).wait_send()
    for cp, cond in pending:
        if cond is None:
            cp.wait_send()
        else:
            pl.when(cond)(cp.wait_send)


def tables():
    half = HEAD_SIZE // 2
    inv_freq = np.exp(np.arange(half) * (-2.0 * math.log(500000.0) / HEAD_SIZE))
    angles = np.arange(SEQUENCE_LENGTH)[:, None] * inv_freq[None, :]
    c, s = np.cos(angles), np.sin(angles)
    cos = np.concatenate([c, c], axis=1).astype(np.float32)
    return cos, np.concatenate([-s, s], axis=1).astype(np.float32)


def whole(D, M, tokens, gain, wq, wk, wv, w_out, final_gain, unembed, clean_ids, corrupt_ids):
    rows, width = tokens.shape
    S = rows // SEQUENCE_LENGTH
    depth = wq.shape[0]
    entries, cols = w_out.shape
    kvw = wk.shape[1] + wv.shape[1]
    total = wq.shape[1] + kvw
    heads, kv_heads = wq.shape[1] // HEAD_SIZE, wk.shape[1] // HEAD_SIZE
    parts = len(spread_plan(D))
    steps = len(spread_plan(D)[0][0])
    sizes = head_groups(heads, depth // parts)
    ngroups = len(sizes) + 1
    xchunks = 2
    half = D // 2
    R = D // M
    cos, sin = tables()
    DMA = pltpu.SemaphoreType.DMA
    ANY = pl.BlockSpec(memory_space=pl.ANY)
    V = pl.BlockSpec(memory_space=pltpu.VMEM)

    def f(*shape):
        return pltpu.VMEM(shape, F32)

    def h(*shape):
        return pltpu.VMEM(shape, BF16)

    I = pl.BlockSpec(memory_space=pltpu.SMEM)
    vocab = unembed.shape[0] if unembed.shape[0] % GROUP == 0 else 0
    if vocab:
        slab = -(-vocab // (4 * GROUP)) * GROUP
        blocks = unembed.reshape(vocab // GROUP, GROUP, width)
        source, source_specs = (blocks, clean_ids, corrupt_ids), [ANY, I, I]
        pages = [h(slab // GROUP, GROUP, width)] * 2
        source_scratch = [f(D, S, width)] + pages + [DMA((4,))]
    else:
        source = (pick(unembed, clean_ids, corrupt_ids).reshape(D, S, width),)
        source_specs, source_scratch = [V], []
    return pl.pallas_call(
        functools.partial(whole_kernel, D, M, sizes, xchunks, rows * D, vocab),
        name="whole",
        out_shape=[
            pltpu.VMEM((rows, entries), BF16),
            pltpu.VMEM((S, heads), F32),
            pltpu.VMEM((S, 1), F32),
        ],
        in_specs=[ANY, V, ANY, ANY, ANY, ANY, ANY, ANY, V] + source_specs,
        out_specs=[V, V, V],
        scratch_shapes=source_scratch + [h(M, width, n) for n in [kvw] + [k * HEAD_SIZE for k in sizes]] + [
            h(M, rows, width), h(M, rows, width), f(rows, total), f(M, 1, width), f(rows, 1),
            f(SEQUENCE_LENGTH, HEAD_SIZE), f(SEQUENCE_LENGTH, HEAD_SIZE),
            h(entries, cols), h(S, 16, width), f(heads // kv_heads, HEAD_SIZE),
            h(S * kv_heads, SEQUENCE_LENGTH, HEAD_SIZE), h(S * kv_heads, SEQUENCE_LENGTH, HEAD_SIZE),
            f(D, S, width), f(R, S, cols), f(D, S, cols), f(R, S, cols), f(D, S, cols),
            f(D, S, entries), f(D, S, entries), f(D * S, entries), f(D * S, entries),
            f(S, entries), f(D, S, entries), f(D * S, entries),
            f(D * S, cols), f(M, D * S, cols), f(D, 4 * S, entries), f(D, 4 * S, entries),
            f(1, entries), f(D, 1, entries),
            DMA((ngroups, parts, 2)), DMA((4 + S,)),
            DMA((M - 1, xchunks, 2)), DMA((M - 1, xchunks, 2)),
            DMA((parts, half, ngroups, steps)), DMA((parts, half, ngroups)),
            DMA((parts, half, ngroups)), DMA((parts, half, ngroups)),
            DMA((D,)), DMA((D,)), DMA((D,)), DMA((D,)), DMA((M,)), DMA((M,)), DMA((D,)), DMA((D,)),
            DMA((R, M)), DMA((D,)), DMA((D,)), DMA((D,)), DMA((D,)), DMA((D,)), DMA((R, M)), DMA((D,)),
        ],
        compiler_params=pltpu.CompilerParams(
            collective_id=0, has_side_effects=True, vmem_limit_bytes=56 * 1024 * 1024
        ),
    )(tokens, gain, wq, wk, wv, jnp.asarray(cos), jnp.asarray(sin), w_out,
      final_gain, *source)


def pick_kernel(per, vocab_rows, clean_ref, corrupt_ref, *refs):
    blocks, out_ref = refs[:-1], refs[-1]
    step = pl.program_id(0)
    start = lax.axis_index("dp") * vocab_rows
    where = lax.broadcasted_iota(jnp.int32, (GROUP, 1), 0)
    for i in range(per):
        rows = []
        for side in range(2):
            at = (clean_ref, corrupt_ref)[side][step * per + i] - start
            block = blocks[side * per + i][...].astype(F32)
            hit = (where == at % GROUP) & (at >= 0) & (at < vocab_rows)
            rows.append(jnp.sum(jnp.where(hit, block, 0.0), axis=0, keepdims=True))
        out_ref[i] = rows[0] - rows[1]


def pick(unembed, clean_ids, corrupt_ids):
    vocab_rows, width = unembed.shape
    n = clean_ids.shape[0]
    per = min(8, n)

    def spec(side, i):
        def index(step, *ids):
            at = ids[side][step * per + i] - lax.axis_index("dp") * vocab_rows
            return jnp.clip(at, 0, vocab_rows - 1) // GROUP, 0
        return pl.BlockSpec((GROUP, width), index)

    return pl.pallas_call(
        functools.partial(pick_kernel, per, vocab_rows),
        name="pick",
        grid_spec=pltpu.PrefetchScalarGridSpec(
            num_scalar_prefetch=2,
            grid=(n // per,),
            in_specs=[spec(side, i) for side in range(2) for i in range(per)],
            out_specs=pl.BlockSpec((per, 1, width), lambda step, *ids: (step, 0, 0)),
        ),
        out_shape=jax.ShapeDtypeStruct((n, 1, width), F32),
    )(clean_ids, corrupt_ids, *([unembed] * (2 * per)))


def settle_kernel(head_ref, scores_ref, metric_ref, head_out, scores_out, metric_out, sem):
    moves = [
        pltpu.make_async_copy(src, dst, sem.at[i])
        for i, (src, dst) in enumerate(
            ((head_ref, head_out), (scores_ref, scores_out), (metric_ref, metric_out))
        )
    ]
    for cp in moves:
        cp.start()
    for cp in moves:
        cp.wait()


def settle(head, scores, metric):
    V = pl.BlockSpec(memory_space=pltpu.VMEM)
    ANY = pl.BlockSpec(memory_space=pl.ANY)
    return pl.pallas_call(
        settle_kernel,
        name="settle",
        out_shape=[jax.ShapeDtypeStruct(x.shape, x.dtype) for x in (head, scores, metric)],
        in_specs=[ANY, ANY, ANY],
        out_specs=[ANY, ANY, ANY],
        scratch_shapes=[pltpu.SemaphoreType.DMA((3,))],
    )(*(pltpu.with_memory_space_constraint(x, pltpu.VMEM) for x in (head, scores, metric)))


def per_device(
    D, M, tokens, attn_gain, w_query, key_w, value_w, w_out, final_gain, unembed,
    clean_ids, corrupt_ids,
):
    S = tokens.shape[0] // SEQUENCE_LENGTH
    head_out, scores, metric = whole(
        D, M, tokens, attn_gain, w_query, key_w, value_w, w_out, final_gain, unembed,
        clean_ids, corrupt_ids,
    )
    head_out, scores, metric = settle(head_out, scores, metric)
    return head_out, scores, metric.reshape(S)


def solution(mesh):
    in_specs = (
        P("dp", "mp"), P(), P("dp", "mp"), P("dp", "mp"), P("dp", "mp"),
        P("mp", "dp"), P("mp"), P("dp", "mp"), P(), P(),
    )
    out_specs = (P("dp", "mp"), P("dp", "mp"), P("dp"))
    return jax.shard_map(
        functools.partial(per_device, mesh.shape["dp"], mesh.shape["mp"]),
        mesh=mesh, in_specs=in_specs, out_specs=out_specs, check_vma=False,
    )
```

```python
import functools
import math

import jax
import jax.numpy as jnp
import numpy as np
from jax import lax
from jax.experimental import pallas as pl
from jax.experimental.pallas import tpu as pltpu
from jax.sharding import PartitionSpec as P

HEAD_SIZE = 128
SEQUENCE_LENGTH = 256
MESH = pl.DeviceIdType.MESH
F32 = jnp.float32
BF16 = jnp.bfloat16
GROUP = 16


def flip(index, mask):
    bit = 1
    out = index
    while bit <= mask:
        if mask & bit:
            out = out + bit - 2 * bit * ((index // bit) % 2)
        bit *= 2
    return out


def spread_plan(size):
    bits = []
    bit = 2
    while bit < size:
        bits.append(bit)
        bit *= 2
    parts = min(2, len(bits))
    plan = []
    for part in range(parts):
        order = bits[part:] + bits[:part]
        held = [0]
        arrivals = []
        for step, b in enumerate(order):
            fresh = [h ^ b for h in held]
            arrivals += [(f, step) for f in fresh]
            held = held + fresh
        plan.append((order, arrivals))
    return plan


def head_groups(heads, piece):
    if piece < 256 or heads < 4:
        return [heads]
    sizes = [2] * ((heads - 4) // 2)
    return sizes + [1] * (heads - sum(sizes))


def order_tasks(events, tasks):
    done = dict(events)
    left = dict(tasks)
    clock = 0.0
    out = []
    while left:
        ready = {
            name: max([0.0] + [done[dep] + lag for dep, lag in deps])
            for name, (deps, dur, rank, fn) in left.items()
            if all(dep in done for dep, lag in deps)
        }
        now = [name for name in ready if ready[name] <= clock]
        if not now:
            clock = min(ready.values())
            continue
        name = min(now, key=lambda n: (left[n][2], ready[n]))
        deps, dur, rank, fn = left.pop(name)
        out.append((clock, fn))
        clock += dur
        done[name] = clock
    return out


def whole_kernel(
    D, M, sizes, xchunks, token_count, vocab,
    tok_ref, gain_ref, wq_ref, wk_ref, wv_ref, cos_hbm, sin_hbm, wout_hbm, fgain_ref, *rest,
):
    if vocab:
        unembed_ref, clean_ref, corrupt_ref = rest[:3]
        head_ref, scores_ref, metric_ref, contrib_ref, slab_a, slab_b, slab_sem = rest[3:10]
        scratch = rest[10:]
    else:
        contrib_ref, head_ref, scores_ref, metric_ref = rest[:4]
        scratch = rest[4:]
    G_ = len(sizes) + 1
    w_bufs = scratch[:G_]
    (
        x_all, x_n, acc, gain_s, gain_v, fgain_v, ss, cos_ref, sin_ref, wout_ref, tail_tok, q_s, k_s, v_s,
        dir_all, g_src, g_all, t_src, t_all, qp_src, qp_all, pre_w, pre_t, last_src, last_all, rows_a,
        out_src, out_all, hg_src, hg_all, tot_src, tot_all,
        far_sem, loc_sem, one_sem, xs_sem, xr_sem, ps_sem, pr_sem, cs_sem, cr_sem,
        s1, r1, s2, r2, s3, r3, s4, r4, s6, r6, s7, r7, s8, r8, s9, r9,
    ) = scratch[G_:]
    d = lax.axis_index("dp")
    m = lax.axis_index("mp")
    plan = spread_plan(D)
    parts = len(plan)
    steps = len(plan[0][0])
    depth = wq_ref.shape[0]
    rows, width = tok_ref.shape
    qw, kw, vw = wq_ref.shape[1], wk_ref.shape[1], wv_ref.shape[1]
    piece = depth // parts
    xpiece = rows // xchunks
    L = SEQUENCE_LENGTH
    S = rows // L
    heads, kv_heads = qw // HEAD_SIZE, kw // HEAD_SIZE
    per_kv = heads // kv_heads
    cols = wout_ref.shape[1]
    R = D // M
    everyone = D * M
    me = d * M + m
    model_width = M * width
    home = d // R
    half = HEAD_SIZE // 2
    DS = D * S

    spans = [(qw, kw + vw)]
    head_span = [None]
    at = 0
    for n in sizes:
        spans.append((at * HEAD_SIZE, n * HEAD_SIZE))
        head_span.append((at, at + n))
        at += n
    ngroups = len(spans)

    def wref(owner, g, p):
        return w_bufs[g].at[owner // R, pl.ds((owner % R) * depth + p * piece, piece), :]

    barrier = pltpu.get_barrier_semaphore()

    bits = []
    while 2 ** len(bits) < D:
        bits.append(2 ** len(bits))

    def tell(sem):
        for near, ok in ((m - 1, m > 0), (m + 1, m < M - 1)):
            @pl.when(ok)
            def _(near=near):
                pl.semaphore_signal(sem, inc=1, device_id=(d, near), device_id_type=MESH)

    beside = jnp.minimum(m, 1) + jnp.minimum(M - 1 - m, 1)

    for bit in bits:
        pl.semaphore_signal(barrier, inc=1, device_id=(flip(d, bit), m), device_id_type=MESH)
    tell(barrier)

    own = {}
    for g in range(ngroups):
        for p in range(parts):
            rr = pl.ds(p * piece, piece)
            dst = wref(d, g, p)
            lo, n = spans[g]
            if g == 0:
                moves = [(wk_ref.at[rr, :], dst.at[:, pl.ds(0, kw)]),
                         (wv_ref.at[rr, :], dst.at[:, pl.ds(kw, vw)])]
            else:
                moves = [(wq_ref.at[rr, pl.ds(lo, n)], dst)]
            own[g, p] = [
                pltpu.make_async_copy(a, b, loc_sem.at[g, p, i]) for i, (a, b) in enumerate(moves)
            ]
            for cp in own[g, p]:
                cp.start()

    xown = pltpu.make_async_copy(tok_ref, x_all.at[m], one_sem.at[0])
    early = [
        pltpu.make_async_copy(cos_hbm, cos_ref, one_sem.at[1]),
        pltpu.make_async_copy(sin_hbm, sin_ref, one_sem.at[2]),
        pltpu.make_async_copy(wout_hbm, wout_ref, one_sem.at[3]),
    ]
    for b in range(S):
        early.append(pltpu.make_async_copy(
            tok_ref.at[pl.ds((b + 1) * L - 16, 16), :], tail_tok.at[b], one_sem.at[4 + b]
        ))
    gains_in = [
        pltpu.make_async_copy(gain_ref, gain_v, one_sem.at[4 + S]),
        pltpu.make_async_copy(fgain_ref, fgain_v, one_sem.at[5 + S]),
    ]
    for cp in early[3:] + gains_in + early[:3]:
        cp.start()
    xown.start()
    ss[...] = jnp.zeros_like(ss)
    pl.semaphore_wait(barrier, len(bits) + beside)

    pending = []
    stamp = [0.0]

    def settle_sends(before):
        while pending and pending[0][0] < before:
            _, cp, cond = pending.pop(0)
            if cond is None:
                cp.wait_send()
            else:
                pl.when(cond)(cp.wait_send)

    def remote(src, dst, send_sem, recv_sem, to, cond=None):
        cp = pltpu.make_async_remote_copy(
            src_ref=src, dst_ref=dst, send_sem=send_sem, recv_sem=recv_sem,
            device_id=to, device_id_type=MESH,
        )
        if cond is None:
            cp.start()
        else:
            pl.when(cond)(cp.start)
        pending.append((stamp[0], cp, cond))

    def local(src, dst, sem, cond=None):
        cp = pltpu.make_async_copy(src, dst, sem)
        if cond is None:
            cp.start()
        else:
            pl.when(cond)(cp.start)

    def arrive(buf, sem, n):
        for i in range(n):
            pltpu.make_async_copy(buf.at[i], buf.at[i], sem.at[i]).wait()

    def spread(src, dst, send_sem, recv_sem, same=False):
        for i in range(1, D):
            to = (d + i) % D
            remote(src if same else src.at[to], dst.at[d], send_sem.at[i], recv_sem.at[d], (to, m))
        local(src if same else src.at[d], dst.at[d], recv_sem.at[d])

    def xsend(hop, c, side):
        rr = pl.ds(c * xpiece, xpiece)
        owner = m - hop if side == 0 else m + hop
        to = m + 1 if side == 0 else m - 1
        return pltpu.make_async_remote_copy(
            src_ref=(tok_ref.at[rr, :] if hop == 0 else x_all.at[owner, rr, :]),
            dst_ref=x_all.at[owner, rr, :],
            send_sem=xs_sem.at[hop, c, side],
            recv_sem=xr_sem.at[hop, c, side],
            device_id=(d, to),
            device_id_type=MESH,
        )

    def xpred(hop, side):
        if side == 0:
            return (m < M - 1) & (m - hop >= 0)
        return (m > 0) & (m + hop < M)

    def xstart(hop, c):
        for side in range(2):
            cp = xsend(hop, c, side)
            pl.when(xpred(hop, side))(cp.start)
            pending.append((stamp[0], cp, xpred(hop, side)))

    def xwait(hop, c):
        rr = pl.ds(c * xpiece, xpiece)
        for side in range(2):
            owner = m - hop - 1 if side == 0 else m + hop + 1
            ok = (m - hop - 1 >= 0) if side == 0 else (m + hop + 1 < M)

            @pl.when(ok)
            def _(side=side, owner=owner):
                pltpu.make_async_copy(
                    x_all.at[owner, rr, :], x_all.at[owner, rr, :], xr_sem.at[hop, c, side]
                ).wait()

    def wcopy(mask, g, p, bit, send_sem, recv_sem):
        ref = wref(flip(d, mask), g, p)
        remote(ref, ref, send_sem, recv_sem, (flip(d, bit), m))

    def wsend(mask, g, p, step):
        bit = plan[p][0][step]
        wcopy(mask, g, p, bit, ps_sem.at[p, mask // 2, g, step],
              pr_sem.at[p, (mask ^ bit) // 2, g])

    def csend(mask, g, p):
        wcopy(mask, g, p, 1, cs_sem.at[p, mask // 2, g], cr_sem.at[p, mask // 2, g])

    def wwait(mask, g, p, sem):
        ref = wref(flip(d, mask), g, p)
        pltpu.make_async_copy(ref, ref, sem).wait()

    def own_ready(g, p):
        for cp in own.pop((g, p), []):
            cp.wait()

    def own_send(g, step):
        for p in range(parts):
            own_ready(g, p)
            wsend(0, g, p, step)
        if step == steps - 1:
            for p in range(parts):
                csend(0, g, p)

    pace = 46e3
    hops = len(plan[0][0])
    rounds = len(plan[0][1])
    shard_time = rows * width * 2 / pace
    group_time = [(D // 2 - 1) * depth * n * 2 / hops / pace for _, n in spans]
    share = hops / rounds
    own_at, rel_at = {}, {}
    clock = 0.0
    queue = []
    for g in range(ngroups):
        queue += [("own", g), ("rel", g)]
    for kind, g in queue:
        if kind == "own":
            own_at[g] = clock
            clock += group_time[g] * share
        else:
            clock += group_time[g] * (1 - share)
            rel_at[g] = clock

    timed = []
    events = {}
    for g in range(ngroups):
        for i in range(rounds):
            alone = [plan[p][1][i][0] & (plan[p][1][i][0] - 1) == 0 for p in range(parts)]
            if all(alone):
                when = own_at[g] + group_time[g] * (plan[0][1][i][1] + 1) / rounds
            else:
                lead = group_time[g] * (rounds - 1 - i) / rounds
                when = rel_at[g] - lead

            def arrival(g=g, i=i):
                for p in range(parts):
                    mask, step = plan[p][1][i]
                    wwait(mask, g, p, pr_sem.at[p, mask // 2, g])
                    for later in range(step + 1, steps):
                        wsend(mask, g, p, later)
                    csend(mask, g, p)

            timed.append((when, 0, len(timed), arrival))
            events["w", g, i] = when
    for h in range(M - 1):
        for c in range(xchunks):
            when = (h + (c + 1) / xchunks) * shard_time

            def xarrival(h=h, c=c):
                xwait(h, c)
                if h + 1 < M - 1:
                    xstart(h + 1, c)

            timed.append((when, 1, len(timed), xarrival))
            events["x", h, c] = when
    xdone = (M - 1) * shard_time
    events["start"] = 0.0

    core_waited = set()

    def partner(g, masks):
        for mask in masks:
            for p in range(parts):
                if (g, mask, p) not in core_waited:
                    core_waited.add((g, mask, p))
                    wwait(mask + 1, g, p, cr_sem.at[p, mask // 2, g])

    begun = set()

    def unit(shard, g, masks):
        partner(g, masks)
        lo, n = spans[g]
        part = jnp.dot(x_n[shard], w_bufs[g][shard], preferred_element_type=F32)
        if g in begun:
            acc[:, lo:lo + n] += part
        else:
            acc[:, lo:lo + n] = part
            begun.add(g)

    evens = list(range(0, D, 2))

    def gained(r):
        if r == 0:
            xown.wait()
        shard = flip(m, r)
        block = 32

        @pl.loop(0, rows // block)
        def _(i):
            rr = pl.ds(pl.multiple_of(i * block, block), block)
            xv = x_all[shard, rr, :].astype(F32)
            ss[rr, :] += jnp.sum(xv * xv, axis=1, keepdims=True)
            x_n[shard, rr, :] = (xv * gain_s[shard]).astype(BF16)

    def inverse_rms():
        ss[...] = lax.rsqrt(ss[...] / model_width + 1e-05)

    def rope(x, cos, sin):
        turned = jnp.concatenate([x[:, half:], x[:, :half]], axis=1)
        return (x * cos + turned * sin).astype(BF16)

    def scores_of(q, k):
        return lax.dot_general(
            q, k, (((1,), (1,)), ((), ())), preferred_element_type=F32
        ) / math.sqrt(HEAD_SIZE)

    def softmax(logits):
        e = jnp.exp(logits - jnp.max(logits, axis=1, keepdims=True))
        return (e * (1.0 / jnp.sum(e, axis=1, keepdims=True))).astype(BF16)

    def fan(src, dst, send_sem, recv_sem):
        for i in range(M - 1, -1, -1):
            k = (m + i) % M
            for jj in range(R):
                to = m * R + jj
                if i == 0:
                    remote(src.at[jj], dst.at[d], send_sem.at[jj, i], recv_sem.at[d], (to, k), to != d)
                    local(src.at[jj], dst.at[d], recv_sem.at[d], to == d)
                else:
                    remote(src.at[jj], dst.at[d], send_sem.at[jj, i], recv_sem.at[d], (to, k))

    slabs = []
    if vocab:
        size = -(-vocab // (4 * GROUP)) * GROUP
        for k, lo in enumerate(range(0, vocab, size)):
            n = min(size, vocab - lo)
            buf = (slab_a, slab_b)[k % 2]
            slabs.append((lo, n, buf, pltpu.make_async_copy(
                unembed_ref.at[pl.ds(lo // GROUP, n // GROUP)], buf.at[pl.ds(0, n // GROUP)],
                slab_sem.at[k],
            )))
    where = lax.broadcasted_iota(jnp.int32, (GROUP, 1), 0)

    def pick_rows(k):
        lo, n, buf, cp = slabs[k]
        cp.wait()
        for i in range(DS):
            picked = []
            for ids in (clean_ref, corrupt_ref):
                at = ids[i] - (d * vocab + lo)
                block = lax.div(jnp.minimum(jnp.maximum(at, 0), n - 1), GROUP)
                got = buf[block].astype(F32)
                hit = where == at - block * GROUP
                picked.append(jnp.sum(jnp.where(hit, got, 0.0), axis=0, keepdims=True))
            row = slice(i % S, i % S + 1)
            if k == 0:
                contrib_ref[i // S, row, :] = picked[0] - picked[1]
            else:
                contrib_ref[i // S, row, :] += picked[0] - picked[1]
        if k + 2 < len(slabs):
            slabs[k + 2][3].start()

    def send_rows():
        spread(contrib_ref, dir_all, s2, r2)

    def first_exchange():
        arrive(dir_all, r2, D)
        direction = dir_all[0]
        for j in range(1, D):
            direction = direction + dir_all[j]
        weighted = fgain_v[...].astype(F32).reshape(1, width) * direction
        for jj in range(R):
            g_src[jj] = weighted[:, jj * cols:(jj + 1) * cols]
        fan(g_src, g_all, s6, r6)

    def joined(buf):
        return jnp.concatenate([buf[j] for j in range(D)], axis=0)

    def last_queries():
        for cp in early[:3]:
            cp.wait()
        arrive(t_all, r9, D)
        block = pl.ds(pl.multiple_of((d % R) * cols, cols), cols)
        lhs = (joined(t_all) * gain_s[home, :, block]).astype(BF16)
        mine = pl.ds((d % R) * depth, depth)
        for g in range(1, ngroups):
            lo, n = spans[g]
            for p in range(parts):
                own_ready(g, p)
            part = jnp.dot(lhs, w_bufs[g][home, mine, :], preferred_element_type=F32)
            for j in range(D):
                qp_src[j, :, lo:lo + n] = part[j * S:(j + 1) * S, :]
        spread(qp_src, qp_all, s8, r8)

    def turned_back(x):
        return lax.dot_general(
            x, wout_ref[...], (((1,), (1,)), ((), ())), preferred_element_type=F32
        )

    def early_grads():
        arrive(g_all, r6, D)
        exact = joined(g_all)
        coarse = exact.astype(BF16)
        fine = (exact - coarse.astype(F32)).astype(BF16)
        pre = turned_back(jnp.concatenate([coarse, fine, joined(t_all).astype(BF16)], axis=0))
        pre_w[...] = pre[:DS] + pre[DS:2 * DS]
        pre_t[...] = pre[2 * DS:]

    def keys_values():
        for b in range(S):
            sb = slice(b * L, (b + 1) * L)
            for n in range(kv_heads):
                lo = qw + n * HEAD_SIZE
                inv = ss[sb, :]
                k_s[b * kv_heads + n] = rope(acc[sb, lo:lo + HEAD_SIZE] * inv, cos_ref[...], sin_ref[...])
                v_s[b * kv_heads + n] = (acc[sb, lo + kw:lo + kw + HEAD_SIZE] * inv).astype(BF16)

    def last_position():
        arrive(qp_all, r8, D)
        q_sum = qp_all[0]
        for j in range(1, D):
            q_sum = q_sum + qp_all[j]
        for b in range(S):
            end = (b + 1) * L - 1
            inv = ss[end:end + 1, :]
            for n in range(kv_heads):
                for g in range(per_kv):
                    h = n * per_kv + g
                    q_s[g:g + 1, :] = q_sum[b:b + 1, h * HEAD_SIZE:(h + 1) * HEAD_SIZE] * inv
                q = rope(q_s[...], cos_ref[L - 1:L, :], sin_ref[L - 1:L, :])
                mixed = jnp.dot(
                    softmax(scores_of(q, k_s[b * kv_heads + n])), v_s[b * kv_heads + n],
                    preferred_element_type=F32,
                ).astype(BF16).astype(F32)
                for g in range(per_kv):
                    h = n * per_kv + g
                    last_src[b:b + 1, h * HEAD_SIZE:(h + 1) * HEAD_SIZE] = mixed[g:g + 1, :]
        spread(last_src, last_all, s1, r1, same=True)

    def project_out():
        arrive(last_all, r1, D)
        for j in range(D):
            rows_a[j * S:(j + 1) * S, :] = last_all[j]
        out_src[...] = jnp.dot(
            rows_a[...].astype(BF16), wout_ref[...], preferred_element_type=F32
        )
        for i in range(1, M):
            to = (m + i) % M
            remote(out_src, out_all.at[m], s3.at[i], r3.at[m], (d, to))
        local(out_src, out_all.at[m], r3.at[m])

    def residual_grads():
        arrive(out_all, r3, M)
        total = out_all[0]
        for k in range(1, M):
            total = total + out_all[k]
        attn = total.astype(BF16)
        residual = joined(t_all) + attn.astype(F32)
        sq = jnp.sum(residual * residual, axis=1, keepdims=True)
        prod = jnp.sum(residual * joined(g_all), axis=1, keepdims=True)
        back = turned_back(attn) + pre_t[...]
        entries = back.shape[1]
        sq = jnp.broadcast_to(sq, (DS, entries))
        prod = jnp.broadcast_to(prod, (DS, entries))
        ahead = pre_w[...]
        for j in range(D):
            sj = slice(j * S, (j + 1) * S)
            hg_src[j, 0:S, :] = ahead[sj]
            hg_src[j, S:2 * S, :] = back[sj]
            hg_src[j, 2 * S:3 * S, :] = sq[sj]
            hg_src[j, 3 * S:4 * S, :] = prod[sj]
        spread(hg_src, hg_all, s7, r7)

    bands = 2
    band = L // bands
    below = (lax.broadcasted_iota(jnp.int32, (band, band), 0)
             >= lax.broadcasted_iota(jnp.int32, (band, band), 1))

    def attend(h):
        at = slice(h * HEAD_SIZE, (h + 1) * HEAD_SIZE)
        for b in range(S):
            n = b * kv_heads + h // per_kv
            sb = slice(b * L, (b + 1) * L)
            q = rope(acc[sb, at] * ss[sb, :], cos_ref[...], sin_ref[...])
            column = None
            for i in range(bands):
                lo, hi = i * band, (i + 1) * band
                logits = scores_of(q[lo:hi], k_s[n, 0:hi, :])
                diag = jnp.where(below, logits[:, lo:hi], -1e30)
                logits = diag if i == 0 else jnp.concatenate([logits[:, :lo], diag], axis=1)
                mixed = jnp.dot(
                    softmax(logits), v_s[n, 0:hi, :], preferred_element_type=F32
                ).astype(BF16)
                head_ref[b * L + lo:b * L + hi, at] = mixed
                part = jnp.sum(mixed.astype(F32), axis=0, keepdims=True)
                column = part if column is None else column + part
            if b == 0:
                tot_src[:, at] = column
            else:
                tot_src[:, at] += column

    def totals():
        spread(tot_src, tot_all, s4, r4, same=True)

    def finish():
        arrive(hg_all, r7, D)
        joint = hg_all[0]
        for j in range(1, D):
            joint = joint + hg_all[j]
        inverse = lax.rsqrt(joint[2 * S:3 * S, :] / model_width + 1e-05)
        metric = inverse * joint[3 * S:4 * S, :]
        metric_ref[...] = metric[:, 0:1]
        fall = metric * inverse * inverse / model_width
        grads = joint[0:S] * inverse - joint[S:2 * S] * fall
        arrive(tot_all, r4, D)
        mean = tot_all[0]
        for j in range(1, D):
            mean = mean + tot_all[j]
        mean = mean / token_count
        gap = (mean - last_src[...]) * grads
        lane = lax.broadcasted_iota(jnp.int32, (S, heads), 1)
        scores = jnp.zeros((S, heads), F32)
        for h in range(heads):
            part = jnp.sum(gap[:, h * HEAD_SIZE:(h + 1) * HEAD_SIZE], axis=1, keepdims=True)
            scores = jnp.where(lane == h, part, scores)
        scores_ref[...] = scores

    tasks = {}
    for r in range(M):
        deps = [("start", 2.0)] if r == 0 else [(("x", r - 1, xchunks - 1), 0.1)]
        tasks["gain", r] = (deps, 1.0, 0, functools.partial(gained, r))
    gains = [(("gain", r), 0.0) for r in range(M)]
    tasks["inv"] = (gains, 0.1, 0, inverse_rms)
    unit_names = {g: [] for g in range(ngroups)}
    for g in range(ngroups):
        cost = 0.25 * spans[g][1] / 128
        late = rel_at[g] > xdone
        for r in range(M):
            if late:
                masks = [k for k in range(D) if k // R == r and k % 2 == 0]
                deps = gains + [
                    (("w", g, i), 1.6) for i in range(rounds)
                    if i == 0 or any(plan[p][1][i][0] in masks for p in range(parts))
                ]
                fn = functools.partial(lambda g, r, ms: unit(flip(home, r), g, ms), g, r, masks)
            else:
                deps = [(("gain", r), 0.0)] + [(("w", g, i), 1.6) for i in range(rounds)]
                fn = functools.partial(lambda g, r: unit(flip(m, r), g, evens), g, r)
            tasks["unit", g, r] = (deps, cost, 1 if g == 0 else 4, fn)
            unit_names[g].append((("unit", g, r), 0.0))
    tasks["kv"] = (unit_names[0] + [("inv", 0.0), ("E3", 0.0)], 1.0, 1, keys_values)
    before = "start"
    for k in range(len(slabs)):
        tasks["pick", k] = ([(before, 4.0)], 1.2, 2, functools.partial(pick_rows, k))
        before = ("pick", k)
    tasks["E1"] = ([(before, 0.0)], 0.1, 2, send_rows)
    tasks["E2"] = ([("E1", 22.0)], 0.5, 2, first_exchange)
    tasks["E3"] = ([("start", 17.0)], 1.0, 2, last_queries)
    tasks["pre"] = ([("E2", 25.0)], 1.0, 5, early_grads)
    tasks["last"] = ([("kv", 0.0), ("E3", 20.0)], 1.5, 1, last_position)
    tasks["T1"] = ([("last", 8.0)], 1.0, 1, project_out)
    tasks["T2"] = ([("T1", 4.0), ("pre", 0.0)], 1.5, 1, residual_grads)
    for g in range(1, ngroups):
        for h in range(*head_span[g]):
            tasks["att", h] = ([("kv", 0.0)] + unit_names[g], 1.2, 6, functools.partial(attend, h))
    tasks["tot"] = ([(("att", h), 0.0) for h in range(heads)], 0.1, 7, totals)
    tasks["fin"] = ([("tot", 0.0), ("T2", 0.0)], 0.1, 8, finish)

    for step in range(steps):
        own_send(0, step)
    xstart(0, 0)
    for i, bit in enumerate(bits):
        pl.semaphore_signal(far_sem.at[i], inc=1, device_id=(flip(d, bit), m), device_id_type=MESH)
        pl.semaphore_wait(far_sem.at[i], 1)
    for i in range(len(bits), len(bits) + M - 1):
        tell(far_sem.at[i])
        pl.semaphore_wait(far_sem.at[i], beside)
    for cp in early[3:] + gains_in:
        cp.wait()
    toks = [tail_tok[b].astype(F32)[15:16, :] for b in range(S)]
    tok = toks[0] if S == 1 else jnp.concatenate(toks, axis=0)
    for jj in range(R):
        t_src[jj] = tok[:, jj * cols:(jj + 1) * cols]
    fan(t_src, t_all, s9, r9)
    for c in range(1, xchunks):
        xstart(0, c)
    for k in range(M):
        gain_s[k] = gain_v[k * width:(k + 1) * width].astype(F32).reshape(1, width)
    for g in range(1, ngroups):
        for step in range(steps):
            when = own_at[g] + group_time[g] * share * step / steps - 4.0
            timed.append((when, -1, len(timed), functools.partial(own_send, g, step)))
    for slab in slabs[:2]:
        slab[3].start()
    ordered = order_tasks(events, tasks)
    timed += [(when, 2, len(timed) + i, fn) for i, (when, fn) in enumerate(ordered)]
    for when, _, _, fn in sorted(timed, key=lambda t: t[:3]):
        stamp[0] = when
        settle_sends(when - 20.0)
        fn()
    for g in range(ngroups):
        partner(g, evens)
    settle_sends(math.inf)


def tables():
    half = HEAD_SIZE // 2
    inv_freq = np.exp(np.arange(half) * (-2.0 * math.log(500000.0) / HEAD_SIZE))
    angles = np.arange(SEQUENCE_LENGTH)[:, None] * inv_freq[None, :]
    c, s = np.cos(angles), np.sin(angles)
    cos = np.concatenate([c, c], axis=1).astype(np.float32)
    return cos, np.concatenate([-s, s], axis=1).astype(np.float32)


def whole(D, M, tokens, gain, wq, wk, wv, w_out, final_gain, unembed, clean_ids, corrupt_ids):
    rows, width = tokens.shape
    S = rows // SEQUENCE_LENGTH
    depth = wq.shape[0]
    entries, cols = w_out.shape
    kvw = wk.shape[1] + wv.shape[1]
    total = wq.shape[1] + kvw
    heads, kv_heads = wq.shape[1] // HEAD_SIZE, wk.shape[1] // HEAD_SIZE
    parts = len(spread_plan(D))
    steps = len(spread_plan(D)[0][0])
    sizes = head_groups(heads, depth // parts)
    ngroups = len(sizes) + 1
    xchunks = 2
    half = D // 2
    R = D // M
    cos, sin = tables()
    DMA = pltpu.SemaphoreType.DMA
    ANY = pl.BlockSpec(memory_space=pl.ANY)
    V = pl.BlockSpec(memory_space=pltpu.VMEM)

    def f(*shape):
        return pltpu.VMEM(shape, F32)

    def h(*shape):
        return pltpu.VMEM(shape, BF16)

    I = pl.BlockSpec(memory_space=pltpu.SMEM)
    vocab = unembed.shape[0] if unembed.shape[0] % GROUP == 0 else 0
    if vocab:
        slab = -(-vocab // (4 * GROUP)) * GROUP
        blocks = unembed.reshape(vocab // GROUP, GROUP, width)
        source, source_specs = (blocks, clean_ids, corrupt_ids), [ANY, I, I]
        pages = [h(slab // GROUP, GROUP, width)] * 2
        source_scratch = [f(D, S, width)] + pages + [DMA((4,))]
    else:
        source = (pick(unembed, clean_ids, corrupt_ids).reshape(D, S, width),)
        source_specs, source_scratch = [V], []
    return pl.pallas_call(
        functools.partial(whole_kernel, D, M, sizes, xchunks, rows * D, vocab),
        name="whole",
        out_shape=[
            pltpu.VMEM((rows, entries), BF16),
            pltpu.VMEM((S, heads), F32),
            pltpu.VMEM((S, 1), F32),
        ],
        in_specs=[ANY] * 9 + source_specs,
        out_specs=[V, V, V],
        scratch_shapes=source_scratch + [h(M, width, n) for n in [kvw] + [k * HEAD_SIZE for k in sizes]] + [
            h(M, rows, width), h(M, rows, width), f(rows, total), f(M, 1, width), h(M * width), h(width), f(rows, 1),
            f(SEQUENCE_LENGTH, HEAD_SIZE), f(SEQUENCE_LENGTH, HEAD_SIZE),
            h(entries, cols), h(S, 16, width), f(heads // kv_heads, HEAD_SIZE),
            h(S * kv_heads, SEQUENCE_LENGTH, HEAD_SIZE), h(S * kv_heads, SEQUENCE_LENGTH, HEAD_SIZE),
            f(D, S, width), f(R, S, cols), f(D, S, cols), f(R, S, cols), f(D, S, cols),
            f(D, S, entries), f(D, S, entries), f(D * S, entries), f(D * S, entries),
            f(S, entries), f(D, S, entries), f(D * S, entries),
            f(D * S, cols), f(M, D * S, cols), f(D, 4 * S, entries), f(D, 4 * S, entries),
            f(1, entries), f(D, 1, entries),
            pltpu.SemaphoreType.REGULAR((D.bit_length() + M,)), DMA((ngroups, parts, 2)), DMA((6 + S,)),
            DMA((M - 1, xchunks, 2)), DMA((M - 1, xchunks, 2)),
            DMA((parts, half, ngroups, steps)), DMA((parts, half, ngroups)),
            DMA((parts, half, ngroups)), DMA((parts, half, ngroups)),
            DMA((D,)), DMA((D,)), DMA((D,)), DMA((D,)), DMA((M,)), DMA((M,)), DMA((D,)), DMA((D,)),
            DMA((R, M)), DMA((D,)), DMA((D,)), DMA((D,)), DMA((D,)), DMA((D,)), DMA((R, M)), DMA((D,)),
        ],
        compiler_params=pltpu.CompilerParams(
            collective_id=0, has_side_effects=True, vmem_limit_bytes=56 * 1024 * 1024
        ),
    )(tokens, gain, wq, wk, wv, jnp.asarray(cos), jnp.asarray(sin), w_out,
      final_gain, *source)


def pick_kernel(per, vocab_rows, clean_ref, corrupt_ref, *refs):
    blocks, out_ref = refs[:-1], refs[-1]
    step = pl.program_id(0)
    start = lax.axis_index("dp") * vocab_rows
    where = lax.broadcasted_iota(jnp.int32, (GROUP, 1), 0)
    for i in range(per):
        rows = []
        for side in range(2):
            at = (clean_ref, corrupt_ref)[side][step * per + i] - start
            block = blocks[side * per + i][...].astype(F32)
            hit = (where == at % GROUP) & (at >= 0) & (at < vocab_rows)
            rows.append(jnp.sum(jnp.where(hit, block, 0.0), axis=0, keepdims=True))
        out_ref[i] = rows[0] - rows[1]


def pick(unembed, clean_ids, corrupt_ids):
    vocab_rows, width = unembed.shape
    n = clean_ids.shape[0]
    per = min(8, n)

    def spec(side, i):
        def index(step, *ids):
            at = ids[side][step * per + i] - lax.axis_index("dp") * vocab_rows
            return jnp.clip(at, 0, vocab_rows - 1) // GROUP, 0
        return pl.BlockSpec((GROUP, width), index)

    return pl.pallas_call(
        functools.partial(pick_kernel, per, vocab_rows),
        name="pick",
        grid_spec=pltpu.PrefetchScalarGridSpec(
            num_scalar_prefetch=2,
            grid=(n // per,),
            in_specs=[spec(side, i) for side in range(2) for i in range(per)],
            out_specs=pl.BlockSpec((per, 1, width), lambda step, *ids: (step, 0, 0)),
        ),
        out_shape=jax.ShapeDtypeStruct((n, 1, width), F32),
    )(clean_ids, corrupt_ids, *([unembed] * (2 * per)))


def settle_kernel(head_ref, scores_ref, metric_ref, head_out, scores_out, metric_out, sem):
    moves = [
        pltpu.make_async_copy(src, dst, sem.at[i])
        for i, (src, dst) in enumerate(
            ((head_ref, head_out), (scores_ref, scores_out), (metric_ref, metric_out))
        )
    ]
    for cp in moves:
        cp.start()
    for cp in moves:
        cp.wait()


def settle(head, scores, metric):
    V = pl.BlockSpec(memory_space=pltpu.VMEM)
    ANY = pl.BlockSpec(memory_space=pl.ANY)
    return pl.pallas_call(
        settle_kernel,
        name="settle",
        out_shape=[jax.ShapeDtypeStruct(x.shape, x.dtype) for x in (head, scores, metric)],
        in_specs=[ANY, ANY, ANY],
        out_specs=[ANY, ANY, ANY],
        scratch_shapes=[pltpu.SemaphoreType.DMA((3,))],
    )(*(pltpu.with_memory_space_constraint(x, pltpu.VMEM) for x in (head, scores, metric)))


def per_device(
    D, M, tokens, attn_gain, w_query, key_w, value_w, w_out, final_gain, unembed,
    clean_ids, corrupt_ids,
):
    S = tokens.shape[0] // SEQUENCE_LENGTH
    head_out, scores, metric = whole(
        D, M, tokens, attn_gain, w_query, key_w, value_w, w_out, final_gain, unembed,
        clean_ids, corrupt_ids,
    )
    head_out, scores, metric = settle(head_out, scores, metric)
    return head_out, scores, metric.reshape(S)


def solution(mesh):
    in_specs = (
        P("dp", "mp"), P(), P("dp", "mp"), P("dp", "mp"), P("dp", "mp"),
        P("mp", "dp"), P("mp"), P("dp", "mp"), P(), P(),
    )
    out_specs = (P("dp", "mp"), P("dp", "mp"), P("dp"))
    return jax.shard_map(
        functools.partial(per_device, mesh.shape["dp"], mesh.shape["mp"]),
        mesh=mesh, in_specs=in_specs, out_specs=out_specs, check_vma=False,
    )
```

```python
import functools
import math

import jax
import jax.numpy as jnp
import numpy as np
from jax import lax
from jax.experimental import pallas as pl
from jax.experimental.pallas import tpu as pltpu
from jax.sharding import PartitionSpec as P

HEAD_SIZE = 128
SEQUENCE_LENGTH = 256
MESH = pl.DeviceIdType.MESH
F32 = jnp.float32
BF16 = jnp.bfloat16
GROUP = 16


def flip(index, mask):
    bit = 1
    out = index
    while bit <= mask:
        if mask & bit:
            out = out + bit - 2 * bit * ((index // bit) % 2)
        bit *= 2
    return out


def spread_plan(size):
    bits = []
    bit = 2
    while bit < size:
        bits.append(bit)
        bit *= 2
    parts = min(2, len(bits))
    plan = []
    for part in range(parts):
        order = bits[part:] + bits[:part]
        held = [0]
        arrivals = []
        for step, b in enumerate(order):
            fresh = [h ^ b for h in held]
            arrivals += [(f, step) for f in fresh]
            held = held + fresh
        plan.append((order, arrivals))
    return plan


def head_groups(heads, piece):
    if piece < 256 or heads < 4:
        return [heads]
    sizes = [2] * ((heads - 4) // 2)
    return sizes + [1] * (heads - sum(sizes))


def order_tasks(events, tasks):
    done = dict(events)
    left = dict(tasks)
    clock = 0.0
    out = []
    while left:
        ready = {
            name: max([0.0] + [done[dep] + lag for dep, lag in deps])
            for name, (deps, dur, rank, fn) in left.items()
            if all(dep in done for dep, lag in deps)
        }
        now = [name for name in ready if ready[name] <= clock]
        if not now:
            clock = min(ready.values())
            continue
        name = min(now, key=lambda n: (left[n][2], ready[n]))
        deps, dur, rank, fn = left.pop(name)
        out.append((clock, fn))
        clock += dur
        done[name] = clock
    return out


def whole_kernel(
    D, M, sizes, xchunks, token_count, vocab,
    tok_ref, gain_ref, wq_ref, wk_ref, wv_ref, cos_hbm, sin_hbm, wout_hbm, fgain_ref, *rest,
):
    if vocab:
        unembed_ref, clean_ref, corrupt_ref = rest[:3]
        head_ref, scores_ref, metric_ref, contrib_ref, slab_a, slab_b, slab_sem = rest[3:10]
        scratch = rest[10:]
    else:
        contrib_ref, head_ref, scores_ref, metric_ref = rest[:4]
        scratch = rest[4:]
    G_ = len(sizes) + 1
    w_bufs = scratch[:G_]
    (
        x_all, x_n, acc, gain_s, gain_v, fgain_v, ss, cos_ref, sin_ref, wout_ref, tail_tok, q_s, k_s, v_s,
        dir_all, g_src, g_all, t_src, t_all, qp_src, qp_all, pre_w, pre_t, last_src, last_all, rows_a,
        out_src, out_all, hg_src, hg_all, tot_src, tot_all,
        far_sem, loc_sem, one_sem, xs_sem, xr_sem, ps_sem, pr_sem, cs_sem, cr_sem,
        s1, r1, s2, r2, s3, r3, s4, r4, s6, r6, s7, r7, s8, r8, s9, r9,
    ) = scratch[G_:]
    d = lax.axis_index("dp")
    m = lax.axis_index("mp")
    plan = spread_plan(D)
    parts = len(plan)
    steps = len(plan[0][0])
    depth = wq_ref.shape[0]
    rows, width = tok_ref.shape
    qw, kw, vw = wq_ref.shape[1], wk_ref.shape[1], wv_ref.shape[1]
    piece = depth // parts
    xpiece = rows // xchunks
    L = SEQUENCE_LENGTH
    S = rows // L
    heads, kv_heads = qw // HEAD_SIZE, kw // HEAD_SIZE
    per_kv = heads // kv_heads
    cols = wout_ref.shape[1]
    R = D // M
    everyone = D * M
    me = d * M + m
    model_width = M * width
    home = d // R
    half = HEAD_SIZE // 2
    DS = D * S

    spans = [(qw, kw + vw)]
    head_span = [None]
    at = 0
    for n in sizes:
        spans.append((at * HEAD_SIZE, n * HEAD_SIZE))
        head_span.append((at, at + n))
        at += n
    ngroups = len(spans)

    def wref(owner, g, p):
        return w_bufs[g].at[owner // R, pl.ds((owner % R) * depth + p * piece, piece), :]

    barrier = pltpu.get_barrier_semaphore()

    bits = []
    while 2 ** len(bits) < D:
        bits.append(2 ** len(bits))

    def tell(sem):
        for near, ok in ((m - 1, m > 0), (m + 1, m < M - 1)):
            @pl.when(ok)
            def _(near=near):
                pl.semaphore_signal(sem, inc=1, device_id=(d, near), device_id_type=MESH)

    beside = jnp.minimum(m, 1) + jnp.minimum(M - 1 - m, 1)

    for bit in bits:
        pl.semaphore_signal(barrier, inc=1, device_id=(flip(d, bit), m), device_id_type=MESH)
    tell(barrier)

    own = {}
    for g in range(ngroups):
        for p in range(parts):
            rr = pl.ds(p * piece, piece)
            dst = wref(d, g, p)
            lo, n = spans[g]
            if g == 0:
                moves = [(wk_ref.at[rr, :], dst.at[:, pl.ds(0, kw)]),
                         (wv_ref.at[rr, :], dst.at[:, pl.ds(kw, vw)])]
            else:
                moves = [(wq_ref.at[rr, pl.ds(lo, n)], dst)]
            own[g, p] = [
                pltpu.make_async_copy(a, b, loc_sem.at[g, p, i]) for i, (a, b) in enumerate(moves)
            ]
            for cp in own[g, p]:
                cp.start()

    xown = pltpu.make_async_copy(tok_ref, x_all.at[m], one_sem.at[0])
    early = [
        pltpu.make_async_copy(cos_hbm, cos_ref, one_sem.at[1]),
        pltpu.make_async_copy(sin_hbm, sin_ref, one_sem.at[2]),
        pltpu.make_async_copy(wout_hbm, wout_ref, one_sem.at[3]),
    ]
    for b in range(S):
        early.append(pltpu.make_async_copy(
            tok_ref.at[pl.ds((b + 1) * L - 16, 16), :], tail_tok.at[b], one_sem.at[4 + b]
        ))
    gains_in = [
        pltpu.make_async_copy(gain_ref, gain_v, one_sem.at[4 + S]),
        pltpu.make_async_copy(fgain_ref, fgain_v, one_sem.at[5 + S]),
    ]
    for cp in early[3:] + gains_in + early[:3]:
        cp.start()
    xown.start()
    ss[...] = jnp.zeros_like(ss)
    pl.semaphore_wait(barrier, len(bits) + beside)

    pending = []
    stamp = [0.0]

    def settle_sends(before):
        while pending and pending[0][0] < before:
            _, cp, cond = pending.pop(0)
            if cond is None:
                cp.wait_send()
            else:
                pl.when(cond)(cp.wait_send)

    def remote(src, dst, send_sem, recv_sem, to, cond=None):
        cp = pltpu.make_async_remote_copy(
            src_ref=src, dst_ref=dst, send_sem=send_sem, recv_sem=recv_sem,
            device_id=to, device_id_type=MESH,
        )
        if cond is None:
            cp.start()
        else:
            pl.when(cond)(cp.start)
        pending.append((stamp[0], cp, cond))

    def local(src, dst, sem, cond=None):
        cp = pltpu.make_async_copy(src, dst, sem)
        if cond is None:
            cp.start()
        else:
            pl.when(cond)(cp.start)

    def arrive(buf, sem, n):
        for i in range(n):
            pltpu.make_async_copy(buf.at[i], buf.at[i], sem.at[i]).wait()

    def spread(src, dst, send_sem, recv_sem, same=False):
        for i in range(1, D):
            to = (d + i) % D
            remote(src if same else src.at[to], dst.at[d], send_sem.at[i], recv_sem.at[d], (to, m))
        local(src if same else src.at[d], dst.at[d], recv_sem.at[d])

    def xsend(hop, c, side):
        rr = pl.ds(c * xpiece, xpiece)
        owner = m - hop if side == 0 else m + hop
        to = m + 1 if side == 0 else m - 1
        return pltpu.make_async_remote_copy(
            src_ref=(tok_ref.at[rr, :] if hop == 0 else x_all.at[owner, rr, :]),
            dst_ref=x_all.at[owner, rr, :],
            send_sem=xs_sem.at[hop, c, side],
            recv_sem=xr_sem.at[hop, c, side],
            device_id=(d, to),
            device_id_type=MESH,
        )

    def xpred(hop, side):
        if side == 0:
            return (m < M - 1) & (m - hop >= 0)
        return (m > 0) & (m + hop < M)

    def xstart(hop, c):
        for side in range(2):
            cp = xsend(hop, c, side)
            pl.when(xpred(hop, side))(cp.start)
            pending.append((stamp[0], cp, xpred(hop, side)))

    def xwait(hop, c):
        rr = pl.ds(c * xpiece, xpiece)
        for side in range(2):
            owner = m - hop - 1 if side == 0 else m + hop + 1
            ok = (m - hop - 1 >= 0) if side == 0 else (m + hop + 1 < M)

            @pl.when(ok)
            def _(side=side, owner=owner):
                pltpu.make_async_copy(
                    x_all.at[owner, rr, :], x_all.at[owner, rr, :], xr_sem.at[hop, c, side]
                ).wait()

    def wcopy(mask, g, p, bit, send_sem, recv_sem):
        ref = wref(flip(d, mask), g, p)
        remote(ref, ref, send_sem, recv_sem, (flip(d, bit), m))

    def wsend(mask, g, p, step):
        bit = plan[p][0][step]
        wcopy(mask, g, p, bit, ps_sem.at[p, mask // 2, g, step],
              pr_sem.at[p, (mask ^ bit) // 2, g])

    def csend(mask, g, p):
        wcopy(mask, g, p, 1, cs_sem.at[p, mask // 2, g], cr_sem.at[p, mask // 2, g])

    def wwait(mask, g, p, sem):
        ref = wref(flip(d, mask), g, p)
        pltpu.make_async_copy(ref, ref, sem).wait()

    def own_ready(g, p):
        for cp in own.pop((g, p), []):
            cp.wait()

    def own_send(g, step):
        for p in range(parts):
            own_ready(g, p)
            wsend(0, g, p, step)
        if step == steps - 1:
            for p in range(parts):
                csend(0, g, p)

    pace = 46e3
    hops = len(plan[0][0])
    rounds = len(plan[0][1])
    shard_time = rows * width * 2 / pace
    group_time = [(D // 2 - 1) * depth * n * 2 / hops / pace for _, n in spans]
    share = hops / rounds
    own_at, rel_at = {}, {}
    clock = 0.0
    queue = []
    for g in range(ngroups):
        queue += [("own", g), ("rel", g)]
    for kind, g in queue:
        if kind == "own":
            own_at[g] = clock
            clock += group_time[g] * share
        else:
            clock += group_time[g] * (1 - share)
            rel_at[g] = clock

    timed = []
    events = {}
    for g in range(ngroups):
        for i in range(rounds):
            alone = [plan[p][1][i][0] & (plan[p][1][i][0] - 1) == 0 for p in range(parts)]
            if all(alone):
                when = own_at[g] + group_time[g] * (plan[0][1][i][1] + 1) / rounds
            else:
                lead = group_time[g] * (rounds - 1 - i) / rounds
                when = rel_at[g] - lead

            def arrival(g=g, i=i):
                for p in range(parts):
                    mask, step = plan[p][1][i]
                    wwait(mask, g, p, pr_sem.at[p, mask // 2, g])
                    for later in range(step + 1, steps):
                        wsend(mask, g, p, later)
                    csend(mask, g, p)

            timed.append((when, 0, len(timed), arrival))
            events["w", g, i] = when
    for h in range(M - 1):
        for c in range(xchunks):
            when = (h + (c + 1) / xchunks) * shard_time

            def xarrival(h=h, c=c):
                xwait(h, c)
                if h + 1 < M - 1:
                    xstart(h + 1, c)

            timed.append((when, 1, len(timed), xarrival))
            events["x", h, c] = when
    xdone = (M - 1) * shard_time
    events["start"] = 0.0

    core_waited = set()

    def partner(g, masks):
        for mask in masks:
            for p in range(parts):
                if (g, mask, p) not in core_waited:
                    core_waited.add((g, mask, p))
                    wwait(mask + 1, g, p, cr_sem.at[p, mask // 2, g])

    begun = set()

    def unit(shard, g, masks):
        partner(g, masks)
        lo, n = spans[g]
        part = jnp.dot(x_n[shard], w_bufs[g][shard], preferred_element_type=F32)
        if g in begun:
            acc[:, lo:lo + n] += part
        else:
            acc[:, lo:lo + n] = part
            begun.add(g)

    evens = list(range(0, D, 2))

    def gained(r, c):
        if r == 0 and c == 0:
            xown.wait()
        shard = flip(m, r)
        block = 32

        @pl.loop(c * xpiece // block, (c + 1) * xpiece // block)
        def _(i):
            rr = pl.ds(pl.multiple_of(i * block, block), block)
            xv = x_all[shard, rr, :].astype(F32)
            ss[rr, :] += jnp.sum(xv * xv, axis=1, keepdims=True)
            x_n[shard, rr, :] = (xv * gain_s[shard]).astype(BF16)

    def inverse_rms():
        ss[...] = lax.rsqrt(ss[...] / model_width + 1e-05)

    def rope(x, cos, sin):
        turned = jnp.concatenate([x[:, half:], x[:, :half]], axis=1)
        return (x * cos + turned * sin).astype(BF16)

    def scores_of(q, k):
        return lax.dot_general(
            q, k, (((1,), (1,)), ((), ())), preferred_element_type=F32
        ) / math.sqrt(HEAD_SIZE)

    def softmax(logits):
        e = jnp.exp(logits - jnp.max(logits, axis=1, keepdims=True))
        return (e * (1.0 / jnp.sum(e, axis=1, keepdims=True))).astype(BF16)

    def fan(src, dst, send_sem, recv_sem):
        for i in range(M - 1, -1, -1):
            k = (m + i) % M
            for jj in range(R):
                to = m * R + jj
                if i == 0:
                    remote(src.at[jj], dst.at[d], send_sem.at[jj, i], recv_sem.at[d], (to, k), to != d)
                    local(src.at[jj], dst.at[d], recv_sem.at[d], to == d)
                else:
                    remote(src.at[jj], dst.at[d], send_sem.at[jj, i], recv_sem.at[d], (to, k))

    slabs = []
    if vocab:
        size = -(-vocab // (4 * GROUP)) * GROUP
        for k, lo in enumerate(range(0, vocab, size)):
            n = min(size, vocab - lo)
            buf = (slab_a, slab_b)[k % 2]
            slabs.append((lo, n, buf, pltpu.make_async_copy(
                unembed_ref.at[pl.ds(lo // GROUP, n // GROUP)], buf.at[pl.ds(0, n // GROUP)],
                slab_sem.at[k],
            )))
    where = lax.broadcasted_iota(jnp.int32, (GROUP, 1), 0)

    def pick_rows(k):
        lo, n, buf, cp = slabs[k]
        cp.wait()
        for i in range(DS):
            picked = []
            for ids in (clean_ref, corrupt_ref):
                at = ids[i] - (d * vocab + lo)
                block = lax.div(jnp.minimum(jnp.maximum(at, 0), n - 1), GROUP)
                got = buf[block].astype(F32)
                hit = where == at - block * GROUP
                picked.append(jnp.sum(jnp.where(hit, got, 0.0), axis=0, keepdims=True))
            row = slice(i % S, i % S + 1)
            if k == 0:
                contrib_ref[i // S, row, :] = picked[0] - picked[1]
            else:
                contrib_ref[i // S, row, :] += picked[0] - picked[1]
        if k + 2 < len(slabs):
            slabs[k + 2][3].start()

    def send_rows():
        spread(contrib_ref, dir_all, s2, r2)

    def first_exchange():
        arrive(dir_all, r2, D)
        direction = dir_all[0]
        for j in range(1, D):
            direction = direction + dir_all[j]
        weighted = fgain_v[...].astype(F32).reshape(1, width) * direction
        for jj in range(R):
            g_src[jj] = weighted[:, jj * cols:(jj + 1) * cols]
        fan(g_src, g_all, s6, r6)

    def joined(buf):
        return jnp.concatenate([buf[j] for j in range(D)], axis=0)

    def last_queries():
        for cp in early[:3]:
            cp.wait()
        arrive(t_all, r9, D)
        block = pl.ds(pl.multiple_of((d % R) * cols, cols), cols)
        lhs = (joined(t_all) * gain_s[home, :, block]).astype(BF16)
        mine = pl.ds((d % R) * depth, depth)
        for g in range(1, ngroups):
            lo, n = spans[g]
            for p in range(parts):
                own_ready(g, p)
            part = jnp.dot(lhs, w_bufs[g][home, mine, :], preferred_element_type=F32)
            for j in range(D):
                qp_src[j, :, lo:lo + n] = part[j * S:(j + 1) * S, :]
        spread(qp_src, qp_all, s8, r8)

    def turned_back(x):
        return lax.dot_general(
            x, wout_ref[...], (((1,), (1,)), ((), ())), preferred_element_type=F32
        )

    def early_grads():
        arrive(g_all, r6, D)
        exact = joined(g_all)
        coarse = exact.astype(BF16)
        fine = (exact - coarse.astype(F32)).astype(BF16)
        pre = turned_back(jnp.concatenate([coarse, fine, joined(t_all).astype(BF16)], axis=0))
        pre_w[...] = pre[:DS] + pre[DS:2 * DS]
        pre_t[...] = pre[2 * DS:]

    def keys_values():
        for b in range(S):
            sb = slice(b * L, (b + 1) * L)
            for n in range(kv_heads):
                lo = qw + n * HEAD_SIZE
                inv = ss[sb, :]
                k_s[b * kv_heads + n] = rope(acc[sb, lo:lo + HEAD_SIZE] * inv, cos_ref[...], sin_ref[...])
                v_s[b * kv_heads + n] = (acc[sb, lo + kw:lo + kw + HEAD_SIZE] * inv).astype(BF16)

    def last_position():
        arrive(qp_all, r8, D)
        q_sum = qp_all[0]
        for j in range(1, D):
            q_sum = q_sum + qp_all[j]
        for b in range(S):
            end = (b + 1) * L - 1
            inv = ss[end:end + 1, :]
            for n in range(kv_heads):
                for g in range(per_kv):
                    h = n * per_kv + g
                    q_s[g:g + 1, :] = q_sum[b:b + 1, h * HEAD_SIZE:(h + 1) * HEAD_SIZE] * inv
                q = rope(q_s[...], cos_ref[L - 1:L, :], sin_ref[L - 1:L, :])
                mixed = jnp.dot(
                    softmax(scores_of(q, k_s[b * kv_heads + n])), v_s[b * kv_heads + n],
                    preferred_element_type=F32,
                ).astype(BF16).astype(F32)
                for g in range(per_kv):
                    h = n * per_kv + g
                    last_src[b:b + 1, h * HEAD_SIZE:(h + 1) * HEAD_SIZE] = mixed[g:g + 1, :]
        spread(last_src, last_all, s1, r1, same=True)

    def project_out():
        arrive(last_all, r1, D)
        for j in range(D):
            rows_a[j * S:(j + 1) * S, :] = last_all[j]
        out_src[...] = jnp.dot(
            rows_a[...].astype(BF16), wout_ref[...], preferred_element_type=F32
        )
        for i in range(1, M):
            to = (m + i) % M
            remote(out_src, out_all.at[m], s3.at[i], r3.at[m], (d, to))
        local(out_src, out_all.at[m], r3.at[m])

    def residual_grads():
        arrive(out_all, r3, M)
        total = out_all[0]
        for k in range(1, M):
            total = total + out_all[k]
        attn = total.astype(BF16)
        residual = joined(t_all) + attn.astype(F32)
        sq = jnp.sum(residual * residual, axis=1, keepdims=True)
        prod = jnp.sum(residual * joined(g_all), axis=1, keepdims=True)
        back = turned_back(attn) + pre_t[...]
        entries = back.shape[1]
        sq = jnp.broadcast_to(sq, (DS, entries))
        prod = jnp.broadcast_to(prod, (DS, entries))
        ahead = pre_w[...]
        for j in range(D):
            sj = slice(j * S, (j + 1) * S)
            hg_src[j, 0:S, :] = ahead[sj]
            hg_src[j, S:2 * S, :] = back[sj]
            hg_src[j, 2 * S:3 * S, :] = sq[sj]
            hg_src[j, 3 * S:4 * S, :] = prod[sj]
        spread(hg_src, hg_all, s7, r7)

    bands = 2
    band = L // bands
    below = (lax.broadcasted_iota(jnp.int32, (band, band), 0)
             >= lax.broadcasted_iota(jnp.int32, (band, band), 1))

    def attend(h):
        at = slice(h * HEAD_SIZE, (h + 1) * HEAD_SIZE)
        for b in range(S):
            n = b * kv_heads + h // per_kv
            sb = slice(b * L, (b + 1) * L)
            q = rope(acc[sb, at] * ss[sb, :], cos_ref[...], sin_ref[...])
            column = None
            for i in range(bands):
                lo, hi = i * band, (i + 1) * band
                logits = scores_of(q[lo:hi], k_s[n, 0:hi, :])
                diag = jnp.where(below, logits[:, lo:hi], -1e30)
                logits = diag if i == 0 else jnp.concatenate([logits[:, :lo], diag], axis=1)
                mixed = jnp.dot(
                    softmax(logits), v_s[n, 0:hi, :], preferred_element_type=F32
                ).astype(BF16)
                head_ref[b * L + lo:b * L + hi, at] = mixed
                part = jnp.sum(mixed.astype(F32), axis=0, keepdims=True)
                column = part if column is None else column + part
            if b == 0:
                tot_src[:, at] = column
            else:
                tot_src[:, at] += column

    def totals():
        spread(tot_src, tot_all, s4, r4, same=True)

    def finish():
        arrive(hg_all, r7, D)
        joint = hg_all[0]
        for j in range(1, D):
            joint = joint + hg_all[j]
        inverse = lax.rsqrt(joint[2 * S:3 * S, :] / model_width + 1e-05)
        metric = inverse * joint[3 * S:4 * S, :]
        metric_ref[...] = metric[:, 0:1]
        fall = metric * inverse * inverse / model_width
        grads = joint[0:S] * inverse - joint[S:2 * S] * fall
        arrive(tot_all, r4, D)
        mean = tot_all[0]
        for j in range(1, D):
            mean = mean + tot_all[j]
        mean = mean / token_count
        gap = (mean - last_src[...]) * grads
        lane = lax.broadcasted_iota(jnp.int32, (S, heads), 1)
        scores = jnp.zeros((S, heads), F32)
        for h in range(heads):
            part = jnp.sum(gap[:, h * HEAD_SIZE:(h + 1) * HEAD_SIZE], axis=1, keepdims=True)
            scores = jnp.where(lane == h, part, scores)
        scores_ref[...] = scores

    tasks = {}
    gain_names = {}
    for r in range(M):
        for c in range(xchunks):
            deps = [("start", 2.0)] if r == 0 else [(("x", r - 1, c), 0.1)]
            if c:
                deps.append((("gain", r, c - 1), 0.0))
            tasks["gain", r, c] = (deps, 1.0 / xchunks, 0, functools.partial(gained, r, c))
        gain_names[r] = [(("gain", r, c), 0.0) for c in range(xchunks)]
    gains = [name for r in range(M) for name in gain_names[r]]
    tasks["inv"] = (gains, 0.1, 0, inverse_rms)
    unit_names = {g: [] for g in range(ngroups)}
    for g in range(ngroups):
        cost = 0.25 * spans[g][1] / 128
        late = rel_at[g] > xdone
        for r in range(M):
            if late:
                masks = [k for k in range(D) if k // R == r and k % 2 == 0]
                deps = gains + [
                    (("w", g, i), 1.6) for i in range(rounds)
                    if i == 0 or any(plan[p][1][i][0] in masks for p in range(parts))
                ]
                fn = functools.partial(lambda g, r, ms: unit(flip(home, r), g, ms), g, r, masks)
            else:
                deps = gain_names[r] + [(("w", g, i), 1.6) for i in range(rounds)]
                fn = functools.partial(lambda g, r: unit(flip(m, r), g, evens), g, r)
            tasks["unit", g, r] = (deps, cost, 1 if g == 0 else 4, fn)
            unit_names[g].append((("unit", g, r), 0.0))
    tasks["kv"] = (unit_names[0] + [("inv", 0.0), ("E3", 0.0)], 1.0, 1, keys_values)
    before = "start"
    for k in range(len(slabs)):
        tasks["pick", k] = ([(before, 4.0)], 1.2, 2, functools.partial(pick_rows, k))
        before = ("pick", k)
    tasks["E1"] = ([(before, 0.0)], 0.1, 2, send_rows)
    tasks["E2"] = ([("E1", 22.0)], 0.5, 2, first_exchange)
    tasks["E3"] = ([("start", 17.0)], 1.0, 2, last_queries)
    tasks["pre"] = ([("E2", 25.0)], 1.0, 5, early_grads)
    tasks["last"] = ([("kv", 0.0), ("E3", 20.0)], 1.5, 1, last_position)
    tasks["T1"] = ([("last", 8.0)], 1.0, 1, project_out)
    tasks["T2"] = ([("T1", 4.0), ("pre", 0.0)], 1.5, 1, residual_grads)
    for g in range(1, ngroups):
        for h in range(*head_span[g]):
            tasks["att", h] = ([("kv", 0.0)] + unit_names[g], 1.2, 6, functools.partial(attend, h))
    tasks["tot"] = ([(("att", h), 0.0) for h in range(heads)], 0.1, 7, totals)
    tasks["fin"] = ([("tot", 0.0), ("T2", 0.0)], 0.1, 8, finish)

    for step in range(steps):
        own_send(0, step)
    xstart(0, 0)
    for i, bit in enumerate(bits):
        pl.semaphore_signal(far_sem.at[i], inc=1, device_id=(flip(d, bit), m), device_id_type=MESH)
        pl.semaphore_wait(far_sem.at[i], 1)
    for i in range(len(bits), len(bits) + M - 1):
        tell(far_sem.at[i])
        pl.semaphore_wait(far_sem.at[i], beside)
    for cp in early[3:] + gains_in:
        cp.wait()
    toks = [tail_tok[b].astype(F32)[15:16, :] for b in range(S)]
    tok = toks[0] if S == 1 else jnp.concatenate(toks, axis=0)
    for jj in range(R):
        t_src[jj] = tok[:, jj * cols:(jj + 1) * cols]
    fan(t_src, t_all, s9, r9)
    for c in range(1, xchunks):
        xstart(0, c)
    for k in range(M):
        gain_s[k] = gain_v[k * width:(k + 1) * width].astype(F32).reshape(1, width)
    for g in range(1, ngroups):
        for step in range(steps):
            when = own_at[g] + group_time[g] * share * step / steps - 3.0
            timed.append((when, -1, len(timed), functools.partial(own_send, g, step)))
    for slab in slabs[:2]:
        slab[3].start()
    ordered = order_tasks(events, tasks)
    timed += [(when, 2, len(timed) + i, fn) for i, (when, fn) in enumerate(ordered)]
    for when, _, _, fn in sorted(timed, key=lambda t: t[:3]):
        stamp[0] = when
        settle_sends(when - 20.0)
        fn()
    for g in range(ngroups):
        partner(g, evens)
    settle_sends(math.inf)


def tables():
    half = HEAD_SIZE // 2
    inv_freq = np.exp(np.arange(half) * (-2.0 * math.log(500000.0) / HEAD_SIZE))
    angles = np.arange(SEQUENCE_LENGTH)[:, None] * inv_freq[None, :]
    c, s = np.cos(angles), np.sin(angles)
    cos = np.concatenate([c, c], axis=1).astype(np.float32)
    return cos, np.concatenate([-s, s], axis=1).astype(np.float32)


def whole(D, M, tokens, gain, wq, wk, wv, w_out, final_gain, unembed, clean_ids, corrupt_ids):
    rows, width = tokens.shape
    S = rows // SEQUENCE_LENGTH
    depth = wq.shape[0]
    entries, cols = w_out.shape
    kvw = wk.shape[1] + wv.shape[1]
    total = wq.shape[1] + kvw
    heads, kv_heads = wq.shape[1] // HEAD_SIZE, wk.shape[1] // HEAD_SIZE
    parts = len(spread_plan(D))
    steps = len(spread_plan(D)[0][0])
    sizes = head_groups(heads, depth // parts)
    ngroups = len(sizes) + 1
    xchunks = 2
    half = D // 2
    R = D // M
    cos, sin = tables()
    DMA = pltpu.SemaphoreType.DMA
    ANY = pl.BlockSpec(memory_space=pl.ANY)
    V = pl.BlockSpec(memory_space=pltpu.VMEM)

    def f(*shape):
        return pltpu.VMEM(shape, F32)

    def h(*shape):
        return pltpu.VMEM(shape, BF16)

    I = pl.BlockSpec(memory_space=pltpu.SMEM)
    vocab = unembed.shape[0] if unembed.shape[0] % GROUP == 0 else 0
    if vocab:
        slab = -(-vocab // (4 * GROUP)) * GROUP
        blocks = unembed.reshape(vocab // GROUP, GROUP, width)
        source, source_specs = (blocks, clean_ids, corrupt_ids), [ANY, I, I]
        pages = [h(slab // GROUP, GROUP, width)] * 2
        source_scratch = [f(D, S, width)] + pages + [DMA((4,))]
    else:
        source = (pick(unembed, clean_ids, corrupt_ids).reshape(D, S, width),)
        source_specs, source_scratch = [V], []
    return pl.pallas_call(
        functools.partial(whole_kernel, D, M, sizes, xchunks, rows * D, vocab),
        name="whole",
        out_shape=[
            pltpu.VMEM((rows, entries), BF16),
            pltpu.VMEM((S, heads), F32),
            pltpu.VMEM((S, 1), F32),
        ],
        in_specs=[ANY] * 9 + source_specs,
        out_specs=[V, V, V],
        scratch_shapes=source_scratch + [h(M, width, n) for n in [kvw] + [k * HEAD_SIZE for k in sizes]] + [
            h(M, rows, width), h(M, rows, width), f(rows, total), f(M, 1, width), h(M * width), h(width), f(rows, 1),
            f(SEQUENCE_LENGTH, HEAD_SIZE), f(SEQUENCE_LENGTH, HEAD_SIZE),
            h(entries, cols), h(S, 16, width), f(heads // kv_heads, HEAD_SIZE),
            h(S * kv_heads, SEQUENCE_LENGTH, HEAD_SIZE), h(S * kv_heads, SEQUENCE_LENGTH, HEAD_SIZE),
            f(D, S, width), f(R, S, cols), f(D, S, cols), f(R, S, cols), f(D, S, cols),
            f(D, S, entries), f(D, S, entries), f(D * S, entries), f(D * S, entries),
            f(S, entries), f(D, S, entries), f(D * S, entries),
            f(D * S, cols), f(M, D * S, cols), f(D, 4 * S, entries), f(D, 4 * S, entries),
            f(1, entries), f(D, 1, entries),
            pltpu.SemaphoreType.REGULAR((D.bit_length() + M,)), DMA((ngroups, parts, 2)), DMA((6 + S,)),
            DMA((M - 1, xchunks, 2)), DMA((M - 1, xchunks, 2)),
            DMA((parts, half, ngroups, steps)), DMA((parts, half, ngroups)),
            DMA((parts, half, ngroups)), DMA((parts, half, ngroups)),
            DMA((D,)), DMA((D,)), DMA((D,)), DMA((D,)), DMA((M,)), DMA((M,)), DMA((D,)), DMA((D,)),
            DMA((R, M)), DMA((D,)), DMA((D,)), DMA((D,)), DMA((D,)), DMA((D,)), DMA((R, M)), DMA((D,)),
        ],
        compiler_params=pltpu.CompilerParams(
            collective_id=0, has_side_effects=True, vmem_limit_bytes=56 * 1024 * 1024
        ),
    )(tokens, gain, wq, wk, wv, jnp.asarray(cos), jnp.asarray(sin), w_out,
      final_gain, *source)


def pick_kernel(per, vocab_rows, clean_ref, corrupt_ref, *refs):
    blocks, out_ref = refs[:-1], refs[-1]
    step = pl.program_id(0)
    start = lax.axis_index("dp") * vocab_rows
    where = lax.broadcasted_iota(jnp.int32, (GROUP, 1), 0)
    for i in range(per):
        rows = []
        for side in range(2):
            at = (clean_ref, corrupt_ref)[side][step * per + i] - start
            block = blocks[side * per + i][...].astype(F32)
            hit = (where == at % GROUP) & (at >= 0) & (at < vocab_rows)
            rows.append(jnp.sum(jnp.where(hit, block, 0.0), axis=0, keepdims=True))
        out_ref[i] = rows[0] - rows[1]


def pick(unembed, clean_ids, corrupt_ids):
    vocab_rows, width = unembed.shape
    n = clean_ids.shape[0]
    per = min(8, n)

    def spec(side, i):
        def index(step, *ids):
            at = ids[side][step * per + i] - lax.axis_index("dp") * vocab_rows
            return jnp.clip(at, 0, vocab_rows - 1) // GROUP, 0
        return pl.BlockSpec((GROUP, width), index)

    return pl.pallas_call(
        functools.partial(pick_kernel, per, vocab_rows),
        name="pick",
        grid_spec=pltpu.PrefetchScalarGridSpec(
            num_scalar_prefetch=2,
            grid=(n // per,),
            in_specs=[spec(side, i) for side in range(2) for i in range(per)],
            out_specs=pl.BlockSpec((per, 1, width), lambda step, *ids: (step, 0, 0)),
        ),
        out_shape=jax.ShapeDtypeStruct((n, 1, width), F32),
    )(clean_ids, corrupt_ids, *([unembed] * (2 * per)))


def settle_kernel(head_ref, scores_ref, metric_ref, head_out, scores_out, metric_out, sem):
    moves = [
        pltpu.make_async_copy(src, dst, sem.at[i])
        for i, (src, dst) in enumerate(
            ((head_ref, head_out), (scores_ref, scores_out), (metric_ref, metric_out))
        )
    ]
    for cp in moves:
        cp.start()
    for cp in moves:
        cp.wait()


def settle(head, scores, metric):
    V = pl.BlockSpec(memory_space=pltpu.VMEM)
    ANY = pl.BlockSpec(memory_space=pl.ANY)
    return pl.pallas_call(
        settle_kernel,
        name="settle",
        out_shape=[jax.ShapeDtypeStruct(x.shape, x.dtype) for x in (head, scores, metric)],
        in_specs=[ANY, ANY, ANY],
        out_specs=[ANY, ANY, ANY],
        scratch_shapes=[pltpu.SemaphoreType.DMA((3,))],
    )(*(pltpu.with_memory_space_constraint(x, pltpu.VMEM) for x in (head, scores, metric)))


def per_device(
    D, M, tokens, attn_gain, w_query, key_w, value_w, w_out, final_gain, unembed,
    clean_ids, corrupt_ids,
):
    S = tokens.shape[0] // SEQUENCE_LENGTH
    head_out, scores, metric = whole(
        D, M, tokens, attn_gain, w_query, key_w, value_w, w_out, final_gain, unembed,
        clean_ids, corrupt_ids,
    )
    head_out, scores, metric = settle(head_out, scores, metric)
    return head_out, scores, metric.reshape(S)


def solution(mesh):
    in_specs = (
        P("dp", "mp"), P(), P("dp", "mp"), P("dp", "mp"), P("dp", "mp"),
        P("mp", "dp"), P("mp"), P("dp", "mp"), P(), P(),
    )
    out_specs = (P("dp", "mp"), P("dp", "mp"), P("dp"))
    return jax.shard_map(
        functools.partial(per_device, mesh.shape["dp"], mesh.shape["mp"]),
        mesh=mesh, in_specs=in_specs, out_specs=out_specs, check_vma=False,
    )
```
